32 devices in a mesh: grp: 2 (over y), blk: 4 (over z), tile: 4 (over x, core).
Axes of the slice: x: 2, y: 2, z: 4, core: 2. Of those that a mesh axis runs over, the one named last changes fastest.
Arguments:
- pieces: bfloat16 [8, 448, 448], P(('grp', 'blk'), 'tile'), parts along dimension 0, may hold values from -6 to 6
- bank: bfloat16 [32, 384, 384], P('blk'), may hold values from -60 to 60
- orient_ids: int32 [8], P('blk'), may hold values from 0 to 7
- defocus_ids: int32 [16], P(('grp', 'blk')), parts along dimension 0, may hold values from 0 to 15
- ctf: bfloat16 [32, 448, 448], P('grp', 'tile'), parts along dimension 0, may hold values from -1 to 1
Outputs:
- best_score: float32 [8, 64, 64], P(('grp', 'blk'), 'tile'), parts along dimension 0
- score_sum: float32 [8, 64, 64], P(('grp', 'blk'), 'tile'), parts along dimension 0
- score_squares: float32 [8, 64, 64], P(('grp', 'blk'), 'tile'), parts along dimension 0
The draws below stay inside these ranges and needn't reach their ends.
There are 2 independent parts, one for each index of `grp`. The reference program is written for one: setup_inputs(seed, part) draws one part's arguments, and reference() takes and returns one part's arrays. A program takes and returns all parts, laid end to end along the dimension named above; an argument that names none is the same for every part. Nothing has to cross between parts.
All inputs are finite; a program needn't handle non-finite values.
Results may differ from the reference program's by a relative error of at most 0.0098.
Values may be sent and summed in bfloat16 or wider, within the bound.
A program may use at most 128 MiB of HBM per device.

```python
import math
import jax
import jax.numpy as jnp
from jax import lax

BOX = 384
LAGS = 64
TMPL_DEV = 2
BANK_DEV = 8
DEFOCI = 16
SIDE = 448
PIECES = 4
TEMPLATES = 8
PROJECTIONS = 32


def draw_bank(key, part):
    key_scale, key_offset, key_values = jax.random.split(jax.random.fold_in(key, 11), 3)
    scale = jnp.exp(jax.random.uniform(key_scale, (PROJECTIONS, 1, 1), jnp.float32, 0.0, math.log(10.0)))
    offset = jax.random.uniform(key_offset, (PROJECTIONS, 1, 1), jnp.float32, -2.0, 2.0) * scale
    values = jnp.clip(jax.random.normal(key_values, (PROJECTIONS, BOX, BOX), jnp.float32), -4.0, 4.0)
    return (values * scale + offset).astype(jnp.bfloat16)


def with_ends(values, key, smallest, high):
    shape = values.shape
    place = [jax.random.randint(jax.random.fold_in(key, axis), (), 0, shape[axis]) for axis in range(len(shape))]
    values = values.at[tuple(place)].set(smallest)
    longest = shape.index(max(shape))
    place[longest] = (place[longest] + 1) % shape[longest]
    return values.at[tuple(place)].set(high)


def block_scale(stream_key, shape, cuts, least, high):
    def one(position, shards_of):
        steps = jax.random.uniform(jax.random.fold_in(jax.random.fold_in(stream_key, 6), position), (shards_of,), jnp.float32, least / len(cuts), high / len(cuts))
        return jnp.repeat(jnp.exp(steps), shape[position] // shards_of).reshape((-1,) + (1,) * (len(shape) - position - 1))

    gain = one(*cuts[0])
    for cut in cuts[1:]:
        gain = gain * one(*cut)
    return gain


def bell_draw(rng, shape, deviation, reach, cuts=(), kind=jnp.bfloat16):
    array = jax.random.normal(rng, shape, jnp.float32) * deviation
    if len(cuts) > 0:
        array = block_scale(rng, shape, cuts, -0.22, 0.18) * array
    return jnp.clip(array, min=-reach, max=reach).astype(kind)


def setup_inputs(seed: int = 0, part: int = 0) -> dict:
    keys = jax.random.split(jax.random.key(seed), 6)
    own_keys = jax.random.split(jax.random.fold_in(keys[5], part), 6)
    return {
        "pieces": bell_draw(own_keys[0], (PIECES, SIDE, SIDE), 1.0, 6.0, ((0, 4), (1, 4))),
        "bank": draw_bank(jax.random.fold_in(keys[5], 71), part),
        "orient_ids": with_ends(jax.random.randint(keys[2], (TEMPLATES,), 0, BANK_DEV), jax.random.fold_in(keys[2], 1), 0, BANK_DEV - 1).astype(jnp.int32),
        "defocus_ids": with_ends(jax.random.randint(own_keys[3], (TEMPLATES,), 0, DEFOCI), jax.random.fold_in(own_keys[3], 1), 0, DEFOCI - 1).astype(jnp.int32),
        "ctf": jnp.clip(jax.random.uniform(own_keys[4], (DEFOCI, SIDE, SIDE), jnp.float32, -1.0, 1.0) * block_scale(own_keys[4], (DEFOCI, SIDE, SIDE), ((1, 4),), -0.4, 0.0), -1.0, 1.0).astype(jnp.bfloat16),
    }


def dft_tables(row_index, col_index, side_len):
    phase_turns = row_index[:, None] * col_index[None, :] % side_len
    phase_angle = phase_turns.astype(jnp.float32) * (2.0 * math.pi / side_len)
    return (jnp.cos(phase_angle).astype(jnp.bfloat16), jnp.sin(phase_angle).astype(jnp.bfloat16))

def rounded(values):
    return lax.optimization_barrier(values.astype(jnp.bfloat16)).astype(jnp.float32)

def reference(pieces, bank, orient_ids, defocus_ids, ctf):
    side_len = SIDE
    all_index = jnp.arange(side_len, dtype=jnp.int32)
    cos_half, sin_half = dft_tables(all_index, all_index, side_len)
    cos_full = cos_half.astype(jnp.float32)
    sin_full = sin_half.astype(jnp.float32)
    owner_index = jnp.arange(TEMPLATES, dtype=jnp.int32) // TMPL_DEV
    chosen = jnp.take(bank, (owner_index * BANK_DEV + orient_ids).astype(jnp.int32), axis=0).astype(jnp.float32)
    centre = lax.optimization_barrier(jnp.mean(chosen, axis=(1, 2), keepdims=True))
    spread = lax.optimization_barrier(jnp.mean((chosen - centre) ** 2, axis=(1, 2), keepdims=True))
    template = rounded((chosen - centre) / (BOX * jnp.sqrt(spread + 1e-05)))
    cos_box = cos_full[:, :BOX]
    sin_box = sin_full[:, :BOX]
    row_re = rounded(jnp.einsum('ka,tab->tkb', cos_box, template))
    row_im = rounded(-jnp.einsum('ka,tab->tkb', sin_box, template))
    full_re = jnp.einsum('tkb,lb->tkl', row_re, cos_box) + jnp.einsum('tkb,lb->tkl', row_im, sin_box)
    full_im = jnp.einsum('tkb,lb->tkl', row_im, cos_box) - jnp.einsum('tkb,lb->tkl', row_re, sin_box)
    gain_sel = jnp.take(ctf, defocus_ids, axis=0).astype(jnp.float32)
    spec_re = rounded(full_re * gain_sel)
    spec_im = rounded(-(full_im * gain_sel))
    cos_lag = cos_full[:, :LAGS]
    sin_lag = sin_full[:, :LAGS]
    cos_out = cos_full[:LAGS, :]
    sin_out = sin_full[:LAGS, :]

    def one_piece(piece_img):
        col_re = rounded(jnp.dot(cos_half, piece_img, preferred_element_type=jnp.float32))
        col_im = rounded(-jnp.dot(sin_half, piece_img, preferred_element_type=jnp.float32))
        mic_re = rounded(jnp.dot(col_re, cos_full, preferred_element_type=jnp.float32) + jnp.dot(col_im, sin_full, preferred_element_type=jnp.float32))
        mic_im = rounded(jnp.dot(col_im, cos_full, preferred_element_type=jnp.float32) - jnp.dot(col_re, sin_full, preferred_element_type=jnp.float32))
        prod_re = rounded(mic_re * spec_re - mic_im * spec_im)
        prod_im = rounded(mic_re * spec_im + mic_im * spec_re)
        lag_re = rounded((jnp.einsum('tkl,lq->tkq', prod_re, cos_lag) - jnp.einsum('tkl,lq->tkq', prod_im, sin_lag)) / side_len)
        lag_im = rounded((jnp.einsum('tkl,lq->tkq', prod_re, sin_lag) + jnp.einsum('tkl,lq->tkq', prod_im, cos_lag)) / side_len)
        correl = (jnp.einsum('pk,tkq->tpq', cos_out, lag_re) - jnp.einsum('pk,tkq->tpq', sin_out, lag_im)) / side_len
        return (lax.optimization_barrier(jnp.max(correl, axis=0)), lax.optimization_barrier(jnp.sum(correl, axis=0)), lax.optimization_barrier(jnp.sum(correl * correl, axis=0)))
    best_score, score_sum, score_squares = lax.map(one_piece, pieces)
    return (best_score, score_sum, score_squares)
```

```python
import functools
import math

import jax
import jax.numpy as jnp
import ml_dtypes
import numpy as np
from jax import lax
from jax.experimental import pallas as pl
from jax.experimental.pallas import tpu as pltpu
from jax.sharding import PartitionSpec as P

MESH = pl.DeviceIdType.MESH
LANES = 128
PARTS = 2


def make_tables(side, box, lags, tiles):
    half = side // 2
    chunk = LANES // 2
    index = np.arange(side)
    angle = (index[:, None] * index[None, :] % side) * (2.0 * math.pi / side)
    cos, sin = np.cos(angle), np.sin(angle)
    over_n = np.zeros((side, tiles, 2, chunk))
    pick = np.zeros((side, tiles, 2, chunk))
    over_l = np.zeros((tiles, 2, 2, chunk, 2, lags))
    for l in range(half + 1):
        t, c = divmod(l, chunk)
        over_n[:, t, 0, c], over_n[:, t, 1, c] = cos[:, l], -sin[:, l]
        pick[l, t, 0, c] = 1.0
        if 0 < l < half:
            pick[side - l, t, 1, c] = 1.0
        for i in range(2):
            over_l[t, i, 0, c, i] = cos[l, :lags]
            over_l[t, i, 1, c, i] = -sin[l, :lags]
    flip = np.zeros((side, side))
    flip[index, -index % side] = 1.0
    tables = (
        over_n.reshape(side, -1),
        np.concatenate([cos, sin]),
        pick.reshape(side, -1),
        flip,
        over_l.reshape(tiles, 4 * chunk, 2 * lags),
    )
    return [jnp.asarray(m.astype(ml_dtypes.bfloat16)) for m in tables]


def dot(a, b):
    return jnp.dot(a, b, preferred_element_type=jnp.float32)


def kernel(
    blks,
    tiles,
    side,
    box,
    lags,
    orient_hbm,
    defocus_hbm,
    piece_hbm,
    bank_hbm,
    ctf_hbm,
    over_n_hbm,
    cs_hbm,
    pick_hbm,
    flip_hbm,
    over_l_hbm,
    out,
    orient,
    defocus,
    piece,
    bank,
    ctf,
    over_n,
    cs,
    pick,
    flip,
    over_l,
    g_out,
    g_in,
    ctf_out,
    ctf_in,
    spec,
    mic,
    cor_out,
    cor_in,
    load_sem,
    g_send,
    g_recv,
    ctf_send,
    ctf_recv,
    mic_send,
    mic_recv,
    relay_send,
    cor_send,
    cor_recv,
):
    b = lax.axis_index("blk")
    t = lax.axis_index("tile")
    rows = side // tiles
    count = spec.shape[0]
    chunk = LANES // 2
    few = blks <= 8
    line = blks == 4
    middle = jnp.logical_or(b == 1, b == 2)
    piece_rows = side // PARTS

    def over(start, stop, body):
        if few:
            for s in range(start, stop):
                body(s)
        else:

            @pl.loop(start, stop)
            def _(s):
                body(s)

    def by_distance(step, sign, far):
        offset = None
        for me in range(blks):
            others = [j for j in range(blks) if j != me]
            others.sort(key=lambda j: abs(j - me), reverse=far)
            value = jnp.int32(sign * (others[step - 1] - me) % blks)
            offset = value if me == 0 else jnp.where(b == me, value, offset)
        return offset

    def swap(x):
        return pltpu.roll(x, chunk, 1)

    names = ("piece", "over_n", "cs", "ctf", "pick", "defocus", "bank", "orient", "flip", "over_l")
    pairs = (
        (piece_hbm.at[0], piece),
        (over_n_hbm, over_n),
        (cs_hbm, cs),
        (ctf_hbm, ctf),
        (pick_hbm, pick),
        (defocus_hbm, defocus),
        (bank_hbm, bank),
        (orient_hbm, orient),
        (flip_hbm, flip),
        (over_l_hbm.at[t], over_l),
    )
    loads = {
        n: pltpu.make_async_copy(p[0], p[1], load_sem.at[i])
        for i, (n, p) in enumerate(zip(names, pairs))
    }
    for n in names[:2]:
        loads[n].start()

    barrier = pltpu.get_barrier_semaphore()
    for dt in range(1, tiles):
        pl.semaphore_signal(
            barrier, inc=1, device_id={"tile": lax.rem(t + dt, tiles)}, device_id_type=MESH
        )

    def greet(s):
        pl.semaphore_signal(
            barrier, inc=1, device_id={"blk": lax.rem(b + s, blks)}, device_id_type=MESH
        )

    over(1, blks, greet)
    for n in names[2:]:
        loads[n].start()

    loads["piece"].wait()
    loads["over_n"].wait()
    spread_out = dot(piece[...], over_n[...]).astype(jnp.bfloat16)
    for to in range(tiles):
        g_out[to] = spread_out[:, to * LANES : (to + 1) * LANES]

    def g_copy(dt, source):
        to = lax.rem(t + dt, tiles)
        return pltpu.make_async_remote_copy(
            src_ref=g_out.at[to],
            dst_ref=g_in.at[source],
            send_sem=g_send.at[dt - 1],
            recv_sem=g_recv.at[dt - 1],
            device_id={"tile": to},
            device_id_type=MESH,
        )

    pl.semaphore_wait(barrier, tiles + blks - 2)
    for dt in range(1, tiles):
        g_copy(dt, t).start()
    g_in[t] = g_out[t]

    loads["cs"].wait()
    for dt in range(1, tiles):
        g_copy(dt, lax.rem(t + tiles - dt, tiles)).wait_recv()
    lane = lax.broadcasted_iota(jnp.int32, (side, LANES), 1)
    real = lane < chunk
    spread_in = g_in[...].reshape(side, LANES)

    def mic_copy(s, slot, h):
        part = mic.at[slot, pl.ds(h * piece_rows, piece_rows)]
        return pltpu.make_async_remote_copy(
            src_ref=part,
            dst_ref=part,
            send_sem=mic_send.at[s - 1, h],
            recv_sem=mic_recv.at[s - 1, h],
            device_id={"blk": lax.rem(b + s, blks)},
            device_id_type=MESH,
        )

    def relay_copy(h):
        part = mic.at[lax.rem(b + 2, blks), pl.ds(h * piece_rows, piece_rows)]
        return pltpu.make_async_remote_copy(
            src_ref=part,
            dst_ref=part,
            send_sem=relay_send.at[h],
            recv_sem=mic_recv.at[jnp.where(b == 2, 2, 0), h],
            device_id={"blk": jnp.where(b == 2, 3, 0)},
            device_id_type=MESH,
        )

    def relay(h):
        if line:

            @pl.when(middle)
            def _():
                mic_copy(2, lax.rem(b + 2, blks), h).wait_recv()
                relay_copy(h).start()

    def to_others(h, act):
        def one_of(s):
            if line and s == 1:

                @pl.when(middle)
                def _():
                    act(mic_copy(by_distance(s, 1, True), b, h))

            else:
                act(mic_copy(by_distance(s, 1, True) if few else s, b, h))

        over(1, blks, one_of)

    for h in range(PARTS):
        low, high = h * piece_rows, (h + 1) * piece_rows
        turned = swap(dot(cs[side + low : side + high], spread_in))
        straight = dot(cs[low:high], spread_in)
        mic[b, low:high] = (straight + jnp.where(real[:piece_rows], turned, -turned)).astype(
            jnp.bfloat16
        )
        to_others(h, lambda c: c.start())

    for n in ("ctf", "pick", "defocus"):
        loads[n].wait()
    for i in range(count):
        taken = dot(ctf[defocus[i]], pick[...]).astype(jnp.bfloat16)
        for to in range(tiles):
            ctf_out[to, i] = taken[:, to * LANES : (to + 1) * LANES]

    def ctf_copy(dt, source):
        to = lax.rem(t + dt, tiles)
        return pltpu.make_async_remote_copy(
            src_ref=ctf_out.at[to],
            dst_ref=ctf_in.at[source],
            send_sem=ctf_send.at[dt - 1],
            recv_sem=ctf_recv.at[dt - 1],
            device_id={"tile": to},
            device_id_type=MESH,
        )

    for dt in range(1, tiles):
        ctf_copy(dt, t).start()
    ctf_in[t] = ctf_out[t]

    loads["bank"].wait()
    loads["orient"].wait()
    columns = over_n[:box, pl.ds(pl.multiple_of(t * LANES, LANES), LANES)]
    firsts = []
    for i in range(count):
        image = bank[orient[i]].astype(jnp.float32)
        centre = jnp.sum(image, keepdims=True) * (1.0 / (box * box))
        image = image - centre
        spread = jnp.sum(image * image, keepdims=True) * (1.0 / (box * box))
        scale = 1.0 / (box * jnp.sqrt(spread + 1e-05))
        template = (image * scale).astype(jnp.bfloat16)
        firsts.append(dot(template, columns).astype(jnp.bfloat16))
    relay(0)
    tmpl = dot(cs[:, :box], jnp.concatenate(firsts, axis=1))

    loads["flip"].wait()
    loads["over_l"].wait()
    for dt in range(1, tiles):
        ctf_copy(dt, lax.rem(t + tiles - dt, tiles)).wait_recv()
    for i in range(count):
        here = ctf_in[:, i].reshape(side, LANES)
        gain = here.astype(jnp.float32) + swap(dot(flip[...], here))
        gain = jnp.where(real, gain, swap(gain))
        part = tmpl[:, i * LANES : (i + 1) * LANES]
        turned = swap(part[side:])
        value = (part[:side] + jnp.where(real, turned, -turned)) * gain
        other = swap(value)
        spec[i, 0] = jnp.where(real, value, other)
        spec[i, 1] = jnp.where(real, other, -value)

    for h in range(1, PARTS):
        relay(h)
    wave = jnp.concatenate([cs[:lags], cs[side : side + lags]], axis=0)
    real_lag = lax.broadcasted_iota(jnp.int32, (lags, LANES), 1) < chunk

    def correlate(slot):
        own = mic[slot].astype(jnp.float32)
        turned = swap(own)
        product = jnp.concatenate(
            [(own * spec[i, 0] + turned * spec[i, 1]).astype(jnp.bfloat16) for i in range(count)],
            axis=1,
        )
        both = dot(wave, product) * (1.0 / side)
        lag = []
        for i in range(count):
            part = both[:, i * LANES : (i + 1) * LANES]
            turned = swap(part[lags:])
            lag.append(part[:lags] + jnp.where(real_lag, -turned, turned))
        lag = jnp.concatenate(lag, axis=1).astype(jnp.bfloat16)
        return dot(lag, over_l[...]).astype(jnp.bfloat16).reshape(tiles, lags // tiles, 2 * lags)

    def cor_copy(s, dt):
        to = lax.rem(t + dt, tiles)
        return pltpu.make_async_remote_copy(
            src_ref=cor_out.at[s, to],
            dst_ref=cor_in.at[s, dt],
            send_sem=cor_send.at[s, dt],
            recv_sem=cor_recv.at[s, dt],
            device_id={"blk": lax.rem(b + blks - s, blks), "tile": to},
            device_id_type=MESH,
        )

    def one(step):
        s = by_distance(step, -1, False) if few else step
        slot = lax.rem(b + blks - s, blks)

        def arrive():
            for h in range(PARTS):
                mic_copy(s, slot, h).wait_recv()

        if line and step == 3:
            pl.when(jnp.logical_not(middle))(arrive)
        else:
            arrive()
        cor_out[s] = correlate(slot)
        for dt in range(tiles):
            cor_copy(s, dt).start()

    cor_out[0] = correlate(b)
    for dt in range(1, tiles):
        cor_copy(0, dt).start()
    cor_in[0, 0] = cor_out[0, t]
    over(1, blks, one)

    for dt in range(1, tiles):
        cor_copy(0, dt).wait_recv()

    def arrived(s):
        for dt in range(tiles):
            cor_copy(s, dt).wait_recv()

    over(1, blks, arrived)
    total = jnp.sum(cor_in[...].astype(jnp.float32), axis=1) * (1.0 / side)
    best = jnp.max(total, axis=0)
    summed = jnp.sum(total, axis=0)
    squares = jnp.sum(total * total, axis=0)
    out[0] = jnp.maximum(best, pltpu.roll(best, lags, 1))[:, :lags]
    out[1] = (summed + pltpu.roll(summed, lags, 1))[:, :lags]
    out[2] = (squares + pltpu.roll(squares, lags, 1))[:, :lags]

    for dt in range(1, tiles):
        g_copy(dt, t).wait_send()
        ctf_copy(dt, t).wait_send()
        cor_copy(0, dt).wait_send()

    def left(s):
        for dt in range(tiles):
            cor_copy(s, dt).wait_send()

    over(1, blks, left)
    for h in range(PARTS):
        to_others(h, lambda c: c.wait_send())
    if line:

        @pl.when(middle)
        def _():
            for h in range(PARTS):
                relay_copy(h).wait_send()


def on_device(blks, tiles, pieces, bank, orient_ids, defocus_ids, ctf):
    side, box = pieces.shape[2], bank.shape[1]
    rows, lags, count = side // tiles, side - box, orient_ids.shape[0]
    tables = make_tables(side, box, lags, tiles)
    over_n, cs, pick, flip, over_l = tables
    bf16, dma = jnp.bfloat16, pltpu.SemaphoreType.DMA
    hbm_spec = pl.BlockSpec(memory_space=pltpu.HBM)
    stats = pl.pallas_call(
        functools.partial(kernel, blks, tiles, side, box, lags),
        out_shape=pltpu.VMEM((3, lags // tiles, lags), jnp.float32),
        in_specs=[hbm_spec] * 10,
        out_specs=pl.BlockSpec(memory_space=pltpu.VMEM),
        scratch_shapes=[
            pltpu.SMEM(orient_ids.shape, jnp.int32),
            pltpu.SMEM(defocus_ids.shape, jnp.int32),
            pltpu.VMEM((rows, side), bf16),
            pltpu.VMEM(bank.shape, bf16),
            pltpu.VMEM(ctf.shape, bf16),
            pltpu.VMEM(over_n.shape, bf16),
            pltpu.VMEM(cs.shape, bf16),
            pltpu.VMEM(pick.shape, bf16),
            pltpu.VMEM(flip.shape, bf16),
            pltpu.VMEM(over_l.shape[1:], bf16),
            pltpu.VMEM((tiles, rows, LANES), bf16),
            pltpu.VMEM((tiles, rows, LANES), bf16),
            pltpu.VMEM((tiles, count, rows, LANES), bf16),
            pltpu.VMEM((tiles, count, rows, LANES), bf16),
            pltpu.VMEM((count, 2, side, LANES), jnp.float32),
            pltpu.VMEM((blks, side, LANES), bf16),
            pltpu.VMEM((blks, tiles, lags // tiles, 2 * lags), bf16),
            pltpu.VMEM((blks, tiles, lags // tiles, 2 * lags), bf16),
            dma((10,)),
            dma((tiles - 1,)),
            dma((tiles - 1,)),
            dma((tiles - 1,)),
            dma((tiles - 1,)),
            dma((blks - 1, PARTS)),
            dma((blks - 1, PARTS)),
            dma((PARTS,)),
            dma((blks, tiles)),
            dma((blks, tiles)),
        ],
        compiler_params=pltpu.CompilerParams(
            collective_id=0, has_side_effects=True, vmem_limit_bytes=56 * 2**20
        ),
    )(orient_ids, defocus_ids, pieces, bank, ctf, *tables)
    return stats[0:1], stats[1:2], stats[2:3]


def solution(mesh):
    blks, tiles = mesh.shape["blk"], mesh.shape["tile"]
    placed = (
        P(("grp", "blk"), "tile", None),
        P("blk", None, None),
        P("blk"),
        P(("grp", "blk")),
        P("grp", "tile", None),
    )
    out = P(("grp", "blk"), "tile", None)
    return jax.shard_map(
        functools.partial(on_device, blks, tiles),
        mesh=mesh,
        in_specs=placed,
        out_specs=(out, out, out),
        check_vma=False,
    )
```

```python
import functools
import math

import jax
import jax.numpy as jnp
import ml_dtypes
import numpy as np
from jax import lax
from jax.experimental import pallas as pl
from jax.experimental.pallas import tpu as pltpu
from jax.sharding import PartitionSpec as P

MESH = pl.DeviceIdType.MESH
LANES = 128
PARTS = 2


def make_tables(side, box, lags, tiles):
    half = side // 2
    chunk = LANES // 2
    index = np.arange(side)
    angle = (index[:, None] * index[None, :] % side) * (2.0 * math.pi / side)
    cos, sin = np.cos(angle), np.sin(angle)
    over_n = np.zeros((side, tiles, 2, chunk))
    pick = np.zeros((side, tiles, 2, chunk))
    over_l = np.zeros((tiles, 2, 2, chunk, 2, lags))
    for l in range(half + 1):
        t, c = divmod(l, chunk)
        over_n[:, t, 0, c], over_n[:, t, 1, c] = cos[:, l], -sin[:, l]
        pick[l, t, 0, c] = 1.0
        if 0 < l < half:
            pick[side - l, t, 1, c] = 1.0
        for i in range(2):
            over_l[t, i, 0, c, i] = cos[l, :lags]
            over_l[t, i, 1, c, i] = -sin[l, :lags]
    flip = np.zeros((side, side))
    flip[index, -index % side] = 1.0
    tables = (
        over_n.reshape(side, -1),
        np.concatenate([cos, sin]),
        pick.reshape(side, -1),
        flip,
        over_l.reshape(tiles, 4 * chunk, 2 * lags),
    )
    return [jnp.asarray(m.astype(ml_dtypes.bfloat16)) for m in tables]


def dot(a, b):
    return jnp.dot(a, b, preferred_element_type=jnp.float32)


def kernel(
    blks,
    tiles,
    side,
    box,
    lags,
    orient_hbm,
    defocus_hbm,
    piece_hbm,
    bank_hbm,
    ctf_hbm,
    over_n_hbm,
    cs_hbm,
    pick_hbm,
    flip_hbm,
    over_l_hbm,
    out,
    orient,
    defocus,
    piece,
    bank,
    ctf,
    over_n,
    cs,
    pick,
    flip,
    over_l,
    g_out,
    g_in,
    ctf_out,
    ctf_in,
    spec,
    mic,
    cor_out,
    cor_in,
    load_sem,
    g_send,
    g_recv,
    ctf_send,
    ctf_recv,
    mic_send,
    mic_recv,
    relay_send,
    cor_send,
    cor_recv,
):
    b = lax.axis_index("blk")
    t = lax.axis_index("tile")
    rows = side // tiles
    count = spec.shape[0]
    chunk = LANES // 2
    few = blks <= 8
    line = blks == 4
    middle = jnp.logical_or(b == 1, b == 2)
    piece_rows = side // PARTS

    def over(start, stop, body):
        if few:
            for s in range(start, stop):
                body(s)
        else:

            @pl.loop(start, stop)
            def _(s):
                body(s)

    def by_distance(step, sign, far):
        offset = None
        for me in range(blks):
            others = [j for j in range(blks) if j != me]
            others.sort(key=lambda j: abs(j - me), reverse=far)
            value = jnp.int32(sign * (others[step - 1] - me) % blks)
            offset = value if me == 0 else jnp.where(b == me, value, offset)
        return offset

    def swap(x):
        return pltpu.roll(x, chunk, 1)

    names = ("piece", "over_n", "cs", "ctf", "pick", "defocus", "bank", "orient", "flip", "over_l")
    pairs = (
        (piece_hbm.at[0], piece),
        (over_n_hbm, over_n),
        (cs_hbm, cs),
        (ctf_hbm, ctf),
        (pick_hbm, pick),
        (defocus_hbm, defocus),
        (bank_hbm, bank),
        (orient_hbm, orient),
        (flip_hbm, flip),
        (over_l_hbm.at[t], over_l),
    )
    loads = {
        n: pltpu.make_async_copy(p[0], p[1], load_sem.at[i])
        for i, (n, p) in enumerate(zip(names, pairs))
    }
    for n in names[:2]:
        loads[n].start()

    barrier = pltpu.get_barrier_semaphore()
    for dt in range(1, tiles):
        pl.semaphore_signal(
            barrier, inc=1, device_id={"tile": lax.rem(t + dt, tiles)}, device_id_type=MESH
        )

    def greet(s):
        pl.semaphore_signal(
            barrier, inc=1, device_id={"blk": lax.rem(b + s, blks)}, device_id_type=MESH
        )

    over(1, blks, greet)
    for n in names[2:]:
        loads[n].start()

    loads["piece"].wait()
    loads["over_n"].wait()
    spread_out = dot(piece[...], over_n[...]).astype(jnp.bfloat16)
    for to in range(tiles):
        g_out[to] = spread_out[:, to * LANES : (to + 1) * LANES]

    def g_copy(dt, source):
        to = lax.rem(t + dt, tiles)
        return pltpu.make_async_remote_copy(
            src_ref=g_out.at[to],
            dst_ref=g_in.at[source],
            send_sem=g_send.at[dt - 1],
            recv_sem=g_recv.at[dt - 1],
            device_id={"tile": to},
            device_id_type=MESH,
        )

    pl.semaphore_wait(barrier, tiles + blks - 2)
    for dt in range(1, tiles):
        g_copy(dt, t).start()
    g_in[t] = g_out[t]

    loads["cs"].wait()
    for dt in range(1, tiles):
        g_copy(dt, lax.rem(t + tiles - dt, tiles)).wait_recv()
    lane = lax.broadcasted_iota(jnp.int32, (side, LANES), 1)
    real = lane < chunk
    spread_in = g_in[...].reshape(side, LANES)

    def mic_copy(s, slot, h):
        part = mic.at[slot, pl.ds(h * piece_rows, piece_rows)]
        return pltpu.make_async_remote_copy(
            src_ref=part,
            dst_ref=part,
            send_sem=mic_send.at[s - 1, h],
            recv_sem=mic_recv.at[s - 1, h],
            device_id={"blk": lax.rem(b + s, blks)},
            device_id_type=MESH,
        )

    def relay_copy(h):
        part = mic.at[lax.rem(b + 2, blks), pl.ds(h * piece_rows, piece_rows)]
        return pltpu.make_async_remote_copy(
            src_ref=part,
            dst_ref=part,
            send_sem=relay_send.at[h],
            recv_sem=mic_recv.at[jnp.where(b == 2, 2, 0), h],
            device_id={"blk": jnp.where(b == 2, 3, 0)},
            device_id_type=MESH,
        )

    def relay(h):
        if line:

            @pl.when(middle)
            def _():
                mic_copy(2, lax.rem(b + 2, blks), h).wait_recv()
                relay_copy(h).start()

    def to_others(h, act):
        def one_of(s):
            if line and s == 1:

                @pl.when(middle)
                def _():
                    act(mic_copy(by_distance(s, 1, True), b, h))

            else:
                act(mic_copy(by_distance(s, 1, True) if few else s, b, h))

        over(1, blks, one_of)

    for h in range(PARTS):
        low, high = h * piece_rows, (h + 1) * piece_rows
        turned = swap(dot(cs[side + low : side + high], spread_in))
        straight = dot(cs[low:high], spread_in)
        mic[b, low:high] = (straight + jnp.where(real[:piece_rows], turned, -turned)).astype(
            jnp.bfloat16
        )
        to_others(h, lambda c: c.start())

    for n in ("ctf", "pick", "defocus"):
        loads[n].wait()
    for i in range(count):
        taken = dot(ctf[defocus[i]], pick[...]).astype(jnp.bfloat16)
        for to in range(tiles):
            ctf_out[to, i] = taken[:, to * LANES : (to + 1) * LANES]

    def ctf_copy(dt, source):
        to = lax.rem(t + dt, tiles)
        return pltpu.make_async_remote_copy(
            src_ref=ctf_out.at[to],
            dst_ref=ctf_in.at[source],
            send_sem=ctf_send.at[dt - 1],
            recv_sem=ctf_recv.at[dt - 1],
            device_id={"tile": to},
            device_id_type=MESH,
        )

    for dt in range(1, tiles):
        ctf_copy(dt, t).start()
    ctf_in[t] = ctf_out[t]

    loads["bank"].wait()
    loads["orient"].wait()
    columns = over_n[:box, pl.ds(pl.multiple_of(t * LANES, LANES), LANES)]
    firsts = []
    for i in range(count):
        image = bank[orient[i]].astype(jnp.float32)
        centre = jnp.sum(image, keepdims=True) * (1.0 / (box * box))
        image = image - centre
        spread = jnp.sum(image * image, keepdims=True) * (1.0 / (box * box))
        scale = 1.0 / (box * jnp.sqrt(spread + 1e-05))
        template = (image * scale).astype(jnp.bfloat16)
        firsts.append(dot(template, columns).astype(jnp.bfloat16))
    relay(0)
    tmpl = dot(cs[:, :box], jnp.concatenate(firsts, axis=1))

    loads["flip"].wait()
    loads["over_l"].wait()
    for dt in range(1, tiles):
        ctf_copy(dt, lax.rem(t + tiles - dt, tiles)).wait_recv()
    for i in range(count):
        here = ctf_in[:, i].reshape(side, LANES)
        gain = here.astype(jnp.float32) + swap(dot(flip[...], here))
        gain = jnp.where(real, gain, swap(gain))
        part = tmpl[:, i * LANES : (i + 1) * LANES]
        turned = swap(part[side:])
        value = (part[:side] + jnp.where(real, turned, -turned)) * gain
        other = swap(value)
        spec[i, 0] = jnp.where(real, value, other)
        spec[i, 1] = jnp.where(real, other, -value)

    for h in range(1, PARTS):
        relay(h)
    wave = jnp.concatenate([cs[:lags], cs[side : side + lags]], axis=0)
    real_lag = lax.broadcasted_iota(jnp.int32, (lags, LANES), 1) < chunk

    def correlate(slot):
        own = mic[slot].astype(jnp.float32)
        turned = swap(own)
        product = jnp.concatenate(
            [(own * spec[i, 0] + turned * spec[i, 1]).astype(jnp.bfloat16) for i in range(count)],
            axis=1,
        )
        both = dot(wave, product) * (1.0 / side)
        lag = []
        for i in range(count):
            part = both[:, i * LANES : (i + 1) * LANES]
            turned = swap(part[lags:])
            lag.append(part[:lags] + jnp.where(real_lag, -turned, turned))
        lag = jnp.concatenate(lag, axis=1).astype(jnp.bfloat16)
        return dot(lag, over_l[...]).astype(jnp.bfloat16).reshape(tiles, lags // tiles, 2 * lags)

    def cor_copy(s, dt):
        to = lax.rem(t + dt, tiles)
        return pltpu.make_async_remote_copy(
            src_ref=cor_out.at[s, to],
            dst_ref=cor_in.at[s, dt],
            send_sem=cor_send.at[s, dt],
            recv_sem=cor_recv.at[s, dt],
            device_id={"blk": lax.rem(b + blks - s, blks), "tile": to},
            device_id_type=MESH,
        )

    def one(step):
        s = by_distance(step, -1, False) if few else step
        slot = lax.rem(b + blks - s, blks)

        def arrive():
            for h in range(PARTS):
                mic_copy(s, slot, h).wait_recv()

        if line and step == 3:
            pl.when(jnp.logical_not(middle))(arrive)
        else:
            arrive()
        cor_out[s] = correlate(slot)
        for dt in range(tiles):
            cor_copy(s, dt).start()

    cor_out[0] = correlate(b)
    for dt in range(1, tiles):
        cor_copy(0, dt).start()
    cor_in[0, 0] = cor_out[0, t]
    over(1, blks, one)

    for dt in range(1, tiles):
        cor_copy(0, dt).wait_recv()

    def arrived(s):
        for dt in range(tiles):
            cor_copy(s, dt).wait_recv()

    over(1, blks, arrived)
    total = jnp.sum(cor_in[...].astype(jnp.float32), axis=1) * (1.0 / side)
    best = jnp.max(total, axis=0)
    summed = jnp.sum(total, axis=0)
    squares = jnp.sum(total * total, axis=0)
    out[0] = jnp.maximum(best, pltpu.roll(best, lags, 1))[:, :lags]
    out[1] = (summed + pltpu.roll(summed, lags, 1))[:, :lags]
    out[2] = (squares + pltpu.roll(squares, lags, 1))[:, :lags]

    for dt in range(1, tiles):
        g_copy(dt, t).wait_send()
        ctf_copy(dt, t).wait_send()
        cor_copy(0, dt).wait_send()

    def left(s):
        for dt in range(tiles):
            cor_copy(s, dt).wait_send()

    over(1, blks, left)
    for h in range(PARTS):
        to_others(h, lambda c: c.wait_send())
    if line:

        @pl.when(middle)
        def _():
            for h in range(PARTS):
                relay_copy(h).wait_send()


def line_kernel(
    side,
    box,
    lags,
    orient_hbm,
    defocus_hbm,
    piece_hbm,
    bank_hbm,
    ctf_hbm,
    over_n_hbm,
    cs_hbm,
    pick_hbm,
    flip_hbm,
    over_l_hbm,
    out,
    orient,
    defocus,
    piece,
    bank,
    ctf,
    over_n,
    cs,
    pick,
    flip,
    over_l,
    g_out,
    g_in,
    ctf_out,
    ctf_in,
    spec,
    mic,
    cor_out,
    cor_in,
    load_sem,
    g_send,
    own_send,
    pass_send,
    g_recv,
    ctf_send,
    ctf_recv,
    relay_send,
    cor_send,
    cor_recv,
):
    blks = tiles = 4
    b = lax.axis_index("blk")
    t = lax.axis_index("tile")
    pair = t + 1 - 2 * lax.rem(t, 2)
    across = lax.rem(t + 2, tiles)
    order = (t, pair, across, lax.rem(pair + 2, tiles))
    mate = b + 1 - 2 * lax.rem(b, 2)
    near = 2 - b // 2
    far = 3 - 3 * (b // 2)
    middle = jnp.logical_or(b == 1, b == 2)
    count = spec.shape[0]
    chunk = LANES // 2

    def swap(x):
        return pltpu.roll(x, chunk, 1)

    names = ("piece", "over_n", "pick", "defocus", "ctf", "bank", "orient", "cs", "flip", "over_l")
    pairs = (
        (piece_hbm.at[0], piece),
        (over_n_hbm, over_n),
        (pick_hbm, pick),
        (defocus_hbm, defocus),
        (ctf_hbm, ctf),
        (bank_hbm, bank),
        (orient_hbm, orient),
        (cs_hbm, cs),
        (flip_hbm, flip),
        (over_l_hbm.at[t], over_l),
    )
    loads = {
        n: pltpu.make_async_copy(p[0], p[1], load_sem.at[i])
        for i, (n, p) in enumerate(zip(names, pairs))
    }
    for n in names[:2]:
        loads[n].start()

    barrier = pltpu.get_barrier_semaphore()

    def greet(level, tos):
        for to in tos:
            pl.semaphore_signal(
                barrier, inc=1, device_id={"blk": level, "tile": to}, device_id_type=MESH
            )

    greet(b, order[1:])

    @pl.when(middle)
    def _():
        greet(near, order[:2])
        greet(far, order[:2])

    greet(mate, order[:2])
    for n in names[2:]:
        loads[n].start()

    with jax.named_scope("w_piece"):
        loads["piece"].wait()
        loads["over_n"].wait()
    spread_out = dot(piece[...], over_n[...]).astype(jnp.bfloat16)
    for to in range(tiles):
        g_out[to] = spread_out[:, to * LANES : (to + 1) * LANES]

    def g_copy(source, src, sem, level, to):
        return pltpu.make_async_remote_copy(
            src_ref=src,
            dst_ref=g_in.at[b, source],
            send_sem=sem,
            recv_sem=g_recv.at[b, source],
            device_id={"blk": level, "tile": to},
            device_id_type=MESH,
        )

    def g_near(i, k):
        to = order[i]
        return g_copy(t, g_out.at[to], g_send.at[i, k], (near, mate)[k], to)

    def g_own(i):
        to = order[i]
        return g_copy(t, g_out.at[to], own_send.at[i - 1], b, to)

    def g_pass(i, k):
        source = order[i]
        return g_copy(source, g_in.at[b, source], pass_send.at[i - 2, k], (near, mate)[k], t)

    def g_sends(act):
        for i in (2, 3):
            act(g_own(i))
        for i in (0, 1):
            for k in range(2):
                act(g_near(i, k))
        act(g_own(1))

    def arrive(j, i):
        part = g_in.at[j, order[i]]
        pltpu.make_async_remote_copy(
            src_ref=part,
            dst_ref=part,
            send_sem=own_send.at[0],
            recv_sem=g_recv.at[j, order[i]],
            device_id={"blk": mate, "tile": t},
            device_id_type=MESH,
        ).wait_recv()

    def relay_copy(k, i):
        j, source = (near, far)[k], order[i]
        part = g_in.at[j, source]
        return pltpu.make_async_remote_copy(
            src_ref=part,
            dst_ref=part,
            send_sem=relay_send.at[k, i],
            recv_sem=g_recv.at[j, source],
            device_id={"blk": mate, "tile": t},
            device_id_type=MESH,
        )

    def relay(k, blocks):
        with jax.named_scope("relay_%d_%d" % (k, blocks[0])):
            @pl.when(middle)
            def _():
                for i in blocks:
                    copy = relay_copy(k, i)
                    copy.wait_recv()
                    copy.start()

    lane = lax.broadcasted_iota(jnp.int32, (side, LANES), 1)
    real = lane < chunk
    with jax.named_scope("w_ctfload"):
        for n in ("ctf", "pick", "defocus"):
            loads[n].wait()
    for i in range(count):
        taken = dot(ctf[defocus[i]], pick[...]).astype(jnp.bfloat16)
        for to in range(tiles):
            ctf_out[to, i] = taken[:, to * LANES : (to + 1) * LANES]

    def ctf_copy(i, source):
        to = order[i]
        return pltpu.make_async_remote_copy(
            src_ref=ctf_out.at[to],
            dst_ref=ctf_in.at[source],
            send_sem=ctf_send.at[i - 1],
            recv_sem=ctf_recv.at[i - 1],
            device_id={"tile": to},
            device_id_type=MESH,
        )

    with jax.named_scope("w_barrier"):
        pl.semaphore_wait(barrier, 7)
    with jax.named_scope("g_sends"):
        g_sends(lambda c: c.start())
        for i in (2, 3, 1):
            ctf_copy(i, t).start()
    g_in[b, t] = g_out[t]
    ctf_in[t] = ctf_out[t]

    with jax.named_scope("w_bank"):
        loads["bank"].wait()
        loads["orient"].wait()
    columns = over_n[:box, pl.ds(pl.multiple_of(t * LANES, LANES), LANES)]
    firsts = []
    for i in range(count):
        image = bank[orient[i]].astype(jnp.float32)
        centre = jnp.sum(image, keepdims=True) * (1.0 / (box * box))
        image = image - centre
        spread = jnp.sum(image * image, keepdims=True) * (1.0 / (box * box))
        scale = 1.0 / (box * jnp.sqrt(spread + 1e-05))
        template = (image * scale).astype(jnp.bfloat16)
        firsts.append(dot(template, columns).astype(jnp.bfloat16))
    with jax.named_scope("pass"):
        for i in (2, 3):
            arrive(b, i)
            for k in range(2):
                g_pass(i, k).start()
    with jax.named_scope("w_cs"):
        loads["cs"].wait()
    tmpl = dot(cs[:, :box], jnp.concatenate(firsts, axis=1))
    relay(0, (0, 1))

    def transform(j):
        spread_in = g_in[j].reshape(side, LANES)
        turned = swap(dot(cs[side:], spread_in))
        straight = dot(cs[:side], spread_in)
        mic[j] = (straight + jnp.where(real, turned, -turned)).astype(jnp.bfloat16)

    with jax.named_scope("w_own"):
        arrive(b, 1)
    with jax.named_scope("t_own"):
        transform(b)
    relay(1, (0, 1))
    relay(0, (2, 3))
    relay(1, (2, 3))
    with jax.named_scope("w_flip"):
        loads["flip"].wait()
        loads["over_l"].wait()
    with jax.named_scope("w_ctf"):
        for i in (1, 2, 3):
            ctf_copy(i, order[i]).wait_recv()
    for i in range(count):
        here = ctf_in[:, i].reshape(side, LANES)
        gain = here.astype(jnp.float32) + swap(dot(flip[...], here))
        gain = jnp.where(real, gain, swap(gain))
        part = tmpl[:, i * LANES : (i + 1) * LANES]
        turned = swap(part[side:])
        value = (part[:side] + jnp.where(real, turned, -turned)) * gain
        other = swap(value)
        spec[i, 0] = jnp.where(real, value, other)
        spec[i, 1] = jnp.where(real, other, -value)

    wave = jnp.concatenate([cs[:lags], cs[side : side + lags]], axis=0)
    real_lag = lax.broadcasted_iota(jnp.int32, (lags, LANES), 1) < chunk

    def correlate(j):
        own = mic[j].astype(jnp.float32)
        turned = swap(own)
        product = jnp.concatenate(
            [(own * spec[i, 0] + turned * spec[i, 1]).astype(jnp.bfloat16) for i in range(count)],
            axis=1,
        )
        both = dot(wave, product) * (1.0 / side)
        lag = []
        for i in range(count):
            part = both[:, i * LANES : (i + 1) * LANES]
            turned = swap(part[lags:])
            lag.append(part[:lags] + jnp.where(real_lag, -turned, turned))
        lag = jnp.concatenate(lag, axis=1).astype(jnp.bfloat16)
        return dot(lag, over_l[...]).astype(jnp.bfloat16).reshape(tiles, lags // tiles, 2 * lags)

    def cor_copy(s, dt):
        to = lax.rem(t + dt, tiles)
        return pltpu.make_async_remote_copy(
            src_ref=cor_out.at[s, to],
            dst_ref=cor_in.at[s, dt],
            send_sem=cor_send.at[s, dt],
            recv_sem=cor_recv.at[s, dt],
            device_id={"blk": lax.rem(b + blks - s, blks), "tile": to},
            device_id_type=MESH,
        )

    def one(j):
        s = lax.rem(b + blks - j, blks)
        cor_out[s] = correlate(j)
        for dt in range(tiles):
            cor_copy(s, dt).start()

    with jax.named_scope("c_own"):
        cor_out[0] = correlate(b)
        for dt in range(1, tiles):
            cor_copy(0, dt).start()
        cor_in[0, 0] = cor_out[0, t]

    second = jnp.where(middle, near, mate)
    third = jnp.where(middle, far, near)
    fourth = jnp.where(middle, mate, far)

    def rest(j, known):
        def wait():
            for i in range(tiles):
                arrive(j, i)

        if known:
            pl.when(jnp.logical_not(middle))(wait)
        else:
            wait()

    with jax.named_scope("w_2"):
        rest(second, True)
    with jax.named_scope("c_2"):
        transform(second)
        one(second)
    with jax.named_scope("w_3"):
        rest(third, True)
    with jax.named_scope("c_3"):
        transform(third)
        one(third)
    with jax.named_scope("w_4"):
        rest(fourth, False)
    with jax.named_scope("c_4"):
        transform(fourth)
        one(fourth)

    with jax.named_scope("w_cor"):
        for s in range(blks):
            for dt in range(0 if s else 1, tiles):
                cor_copy(s, dt).wait_recv()
    with jax.named_scope("final"):
        total = jnp.sum(cor_in[...].astype(jnp.float32), axis=1) * (1.0 / side)
        best = jnp.max(total, axis=0)
        summed = jnp.sum(total, axis=0)
        squares = jnp.sum(total * total, axis=0)
        out[0] = jnp.maximum(best, pltpu.roll(best, lags, 1))[:, :lags]
        out[1] = (summed + pltpu.roll(summed, lags, 1))[:, :lags]
        out[2] = (squares + pltpu.roll(squares, lags, 1))[:, :lags]

    with jax.named_scope("w_send"):
        g_sends(lambda c: c.wait_send())
        for i in (1, 2, 3):
            ctf_copy(i, t).wait_send()
        for i in (2, 3):
            for k in range(2):
                g_pass(i, k).wait_send()
        for s in range(blks):
            for dt in range(0 if s else 1, tiles):
                cor_copy(s, dt).wait_send()

        @pl.when(middle)
        def _():
            for k in range(2):
                for i in range(tiles):
                    relay_copy(k, i).wait_send()


def on_device(blks, tiles, pieces, bank, orient_ids, defocus_ids, ctf):
    side, box = pieces.shape[2], bank.shape[1]
    rows, lags, count = side // tiles, side - box, orient_ids.shape[0]
    tables = make_tables(side, box, lags, tiles)
    over_n, cs, pick, flip, over_l = tables
    bf16, dma = jnp.bfloat16, pltpu.SemaphoreType.DMA
    hbm_spec = pl.BlockSpec(memory_space=pltpu.HBM)
    line = blks == 4 and tiles == 4
    loaded = [
        pltpu.SMEM(orient_ids.shape, jnp.int32),
        pltpu.SMEM(defocus_ids.shape, jnp.int32),
        pltpu.VMEM((rows, side), bf16),
        pltpu.VMEM(bank.shape, bf16),
        pltpu.VMEM(ctf.shape, bf16),
        pltpu.VMEM(over_n.shape, bf16),
        pltpu.VMEM(cs.shape, bf16),
        pltpu.VMEM(pick.shape, bf16),
        pltpu.VMEM(flip.shape, bf16),
        pltpu.VMEM(over_l.shape[1:], bf16),
    ]
    gain = [pltpu.VMEM((tiles, count, rows, LANES), bf16)] * 2
    spec = pltpu.VMEM((count, 2, side, LANES), jnp.float32)
    cor = [pltpu.VMEM((blks, tiles, lags // tiles, 2 * lags), bf16)] * 2
    if line:
        body = functools.partial(line_kernel, side, box, lags)
        scratch = [
            *loaded,
            pltpu.VMEM((tiles, rows, LANES), bf16),
            pltpu.VMEM((blks, tiles, rows, LANES), bf16),
            *gain,
            spec,
            pltpu.VMEM((blks, side, LANES), bf16),
            *cor,
            dma((10,)),
            dma((2, 2)),
            dma((3,)),
            dma((2, 2)),
            dma((blks, tiles)),
            dma((tiles - 1,)),
            dma((tiles - 1,)),
            dma((2, tiles)),
            dma((blks, tiles)),
            dma((blks, tiles)),
        ]
    else:
        body = functools.partial(kernel, blks, tiles, side, box, lags)
        scratch = [
            *loaded,
            pltpu.VMEM((tiles, rows, LANES), bf16),
            pltpu.VMEM((tiles, rows, LANES), bf16),
            *gain,
            spec,
            pltpu.VMEM((blks, side, LANES), bf16),
            *cor,
            dma((10,)),
            dma((tiles - 1,)),
            dma((tiles - 1,)),
            dma((tiles - 1,)),
            dma((tiles - 1,)),
            dma((blks - 1, PARTS)),
            dma((blks - 1, PARTS)),
            dma((PARTS,)),
            dma((blks, tiles)),
            dma((blks, tiles)),
        ]
    stats = pl.pallas_call(
        body,
        out_shape=pltpu.VMEM((3, lags // tiles, lags), jnp.float32),
        in_specs=[hbm_spec] * 10,
        out_specs=pl.BlockSpec(memory_space=pltpu.VMEM),
        scratch_shapes=scratch,
        compiler_params=pltpu.CompilerParams(
            collective_id=0, has_side_effects=True, vmem_limit_bytes=56 * 2**20
        ),
    )(orient_ids, defocus_ids, pieces, bank, ctf, *tables)
    return stats[0:1], stats[1:2], stats[2:3]


def solution(mesh):
    blks, tiles = mesh.shape["blk"], mesh.shape["tile"]
    placed = (
        P(("grp", "blk"), "tile", None),
        P("blk", None, None),
        P("blk"),
        P(("grp", "blk")),
        P("grp", "tile", None),
    )
    out = P(("grp", "blk"), "tile", None)
    return jax.shard_map(
        functools.partial(on_device, blks, tiles),
        mesh=mesh,
        in_specs=placed,
        out_specs=(out, out, out),
        check_vma=False,
    )
```

```python
import functools
import math

import jax
import jax.numpy as jnp
import ml_dtypes
import numpy as np
from jax import lax
from jax.experimental import pallas as pl
from jax.experimental.pallas import tpu as pltpu
from jax.sharding import PartitionSpec as P

MESH = pl.DeviceIdType.MESH
LANES = 128
PARTS = 2


def make_tables(side, box, lags, tiles):
    half = side // 2
    chunk = LANES // 2
    index = np.arange(side)
    angle = (index[:, None] * index[None, :] % side) * (2.0 * math.pi / side)
    cos, sin = np.cos(angle), np.sin(angle)
    over_n = np.zeros((side, tiles, 2, chunk))
    pick = np.zeros((side, tiles, 2, chunk))
    over_l = np.zeros((tiles, 2, 2, chunk, 2, lags))
    for l in range(half + 1):
        t, c = divmod(l, chunk)
        over_n[:, t, 0, c], over_n[:, t, 1, c] = cos[:, l], -sin[:, l]
        pick[l, t, 0, c] = 1.0
        if 0 < l < half:
            pick[side - l, t, 1, c] = 1.0
        for i in range(2):
            over_l[t, i, 0, c, i] = cos[l, :lags]
            over_l[t, i, 1, c, i] = -sin[l, :lags]
    flip = np.zeros((side, side))
    flip[index, -index % side] = 1.0
    tables = (
        over_n.reshape(side, -1),
        np.concatenate([cos, sin]),
        pick.reshape(side, -1),
        flip,
        over_l.reshape(tiles, 4 * chunk, 2 * lags),
    )
    return [jnp.asarray(m.astype(ml_dtypes.bfloat16)) for m in tables]


def dot(a, b):
    return jnp.dot(a, b, preferred_element_type=jnp.float32)


def kernel(
    blks,
    tiles,
    side,
    box,
    lags,
    orient_hbm,
    defocus_hbm,
    piece_hbm,
    bank_hbm,
    ctf_hbm,
    over_n_hbm,
    cs_hbm,
    pick_hbm,
    flip_hbm,
    over_l_hbm,
    out,
    orient,
    defocus,
    piece,
    bank,
    ctf,
    over_n,
    cs,
    pick,
    flip,
    over_l,
    g_out,
    g_in,
    ctf_out,
    ctf_in,
    spec,
    mic,
    cor_out,
    cor_in,
    load_sem,
    g_send,
    g_recv,
    ctf_send,
    ctf_recv,
    mic_send,
    mic_recv,
    relay_send,
    cor_send,
    cor_recv,
):
    b = lax.axis_index("blk")
    t = lax.axis_index("tile")
    rows = side // tiles
    count = spec.shape[0]
    chunk = LANES // 2
    few = blks <= 8
    line = blks == 4
    middle = jnp.logical_or(b == 1, b == 2)
    piece_rows = side // PARTS

    def over(start, stop, body):
        if few:
            for s in range(start, stop):
                body(s)
        else:

            @pl.loop(start, stop)
            def _(s):
                body(s)

    def by_distance(step, sign, far):
        offset = None
        for me in range(blks):
            others = [j for j in range(blks) if j != me]
            others.sort(key=lambda j: abs(j - me), reverse=far)
            value = jnp.int32(sign * (others[step - 1] - me) % blks)
            offset = value if me == 0 else jnp.where(b == me, value, offset)
        return offset

    def swap(x):
        return pltpu.roll(x, chunk, 1)

    names = ("piece", "over_n", "cs", "ctf", "pick", "defocus", "bank", "orient", "flip", "over_l")
    pairs = (
        (piece_hbm.at[0], piece),
        (over_n_hbm, over_n),
        (cs_hbm, cs),
        (ctf_hbm, ctf),
        (pick_hbm, pick),
        (defocus_hbm, defocus),
        (bank_hbm, bank),
        (orient_hbm, orient),
        (flip_hbm, flip),
        (over_l_hbm.at[t], over_l),
    )
    loads = {
        n: pltpu.make_async_copy(p[0], p[1], load_sem.at[i])
        for i, (n, p) in enumerate(zip(names, pairs))
    }
    for n in names[:2]:
        loads[n].start()

    barrier = pltpu.get_barrier_semaphore()
    for dt in range(1, tiles):
        pl.semaphore_signal(
            barrier, inc=1, device_id={"tile": lax.rem(t + dt, tiles)}, device_id_type=MESH
        )

    def greet(s):
        pl.semaphore_signal(
            barrier, inc=1, device_id={"blk": lax.rem(b + s, blks)}, device_id_type=MESH
        )

    over(1, blks, greet)
    for n in names[2:]:
        loads[n].start()

    loads["piece"].wait()
    loads["over_n"].wait()
    spread_out = dot(piece[...], over_n[...]).astype(jnp.bfloat16)
    for to in range(tiles):
        g_out[to] = spread_out[:, to * LANES : (to + 1) * LANES]

    def g_copy(dt, source):
        to = lax.rem(t + dt, tiles)
        return pltpu.make_async_remote_copy(
            src_ref=g_out.at[to],
            dst_ref=g_in.at[source],
            send_sem=g_send.at[dt - 1],
            recv_sem=g_recv.at[dt - 1],
            device_id={"tile": to},
            device_id_type=MESH,
        )

    pl.semaphore_wait(barrier, tiles + blks - 2)
    for dt in range(1, tiles):
        g_copy(dt, t).start()
    g_in[t] = g_out[t]

    loads["cs"].wait()
    for dt in range(1, tiles):
        g_copy(dt, lax.rem(t + tiles - dt, tiles)).wait_recv()
    lane = lax.broadcasted_iota(jnp.int32, (side, LANES), 1)
    real = lane < chunk
    spread_in = g_in[...].reshape(side, LANES)

    def mic_copy(s, slot, h):
        part = mic.at[slot, pl.ds(h * piece_rows, piece_rows)]
        return pltpu.make_async_remote_copy(
            src_ref=part,
            dst_ref=part,
            send_sem=mic_send.at[s - 1, h],
            recv_sem=mic_recv.at[s - 1, h],
            device_id={"blk": lax.rem(b + s, blks)},
            device_id_type=MESH,
        )

    def relay_copy(h):
        part = mic.at[lax.rem(b + 2, blks), pl.ds(h * piece_rows, piece_rows)]
        return pltpu.make_async_remote_copy(
            src_ref=part,
            dst_ref=part,
            send_sem=relay_send.at[h],
            recv_sem=mic_recv.at[jnp.where(b == 2, 2, 0), h],
            device_id={"blk": jnp.where(b == 2, 3, 0)},
            device_id_type=MESH,
        )

    def relay(h):
        if line:

            @pl.when(middle)
            def _():
                mic_copy(2, lax.rem(b + 2, blks), h).wait_recv()
                relay_copy(h).start()

    def to_others(h, act):
        def one_of(s):
            if line and s == 1:

                @pl.when(middle)
                def _():
                    act(mic_copy(by_distance(s, 1, True), b, h))

            else:
                act(mic_copy(by_distance(s, 1, True) if few else s, b, h))

        over(1, blks, one_of)

    for h in range(PARTS):
        low, high = h * piece_rows, (h + 1) * piece_rows
        turned = swap(dot(cs[side + low : side + high], spread_in))
        straight = dot(cs[low:high], spread_in)
        mic[b, low:high] = (straight + jnp.where(real[:piece_rows], turned, -turned)).astype(
            jnp.bfloat16
        )
        to_others(h, lambda c: c.start())

    for n in ("ctf", "pick", "defocus"):
        loads[n].wait()
    for i in range(count):
        taken = dot(ctf[defocus[i]], pick[...]).astype(jnp.bfloat16)
        for to in range(tiles):
            ctf_out[to, i] = taken[:, to * LANES : (to + 1) * LANES]

    def ctf_copy(dt, source):
        to = lax.rem(t + dt, tiles)
        return pltpu.make_async_remote_copy(
            src_ref=ctf_out.at[to],
            dst_ref=ctf_in.at[source],
            send_sem=ctf_send.at[dt - 1],
            recv_sem=ctf_recv.at[dt - 1],
            device_id={"tile": to},
            device_id_type=MESH,
        )

    for dt in range(1, tiles):
        ctf_copy(dt, t).start()
    ctf_in[t] = ctf_out[t]

    loads["bank"].wait()
    loads["orient"].wait()
    columns = over_n[:box, pl.ds(pl.multiple_of(t * LANES, LANES), LANES)]
    firsts = []
    for i in range(count):
        image = bank[orient[i]].astype(jnp.float32)
        centre = jnp.sum(image, keepdims=True) * (1.0 / (box * box))
        image = image - centre
        spread = jnp.sum(image * image, keepdims=True) * (1.0 / (box * box))
        scale = 1.0 / (box * jnp.sqrt(spread + 1e-05))
        template = (image * scale).astype(jnp.bfloat16)
        firsts.append(dot(template, columns).astype(jnp.bfloat16))
    relay(0)
    tmpl = dot(cs[:, :box], jnp.concatenate(firsts, axis=1))

    loads["flip"].wait()
    loads["over_l"].wait()
    for dt in range(1, tiles):
        ctf_copy(dt, lax.rem(t + tiles - dt, tiles)).wait_recv()
    for i in range(count):
        here = ctf_in[:, i].reshape(side, LANES)
        gain = here.astype(jnp.float32) + swap(dot(flip[...], here))
        gain = jnp.where(real, gain, swap(gain))
        part = tmpl[:, i * LANES : (i + 1) * LANES]
        turned = swap(part[side:])
        value = (part[:side] + jnp.where(real, turned, -turned)) * gain
        other = swap(value)
        spec[i, 0] = jnp.where(real, value, other)
        spec[i, 1] = jnp.where(real, other, -value)

    for h in range(1, PARTS):
        relay(h)
    wave = jnp.concatenate([cs[:lags], cs[side : side + lags]], axis=0)
    real_lag = lax.broadcasted_iota(jnp.int32, (lags, LANES), 1) < chunk

    def correlate(slot):
        own = mic[slot].astype(jnp.float32)
        turned = swap(own)
        product = jnp.concatenate(
            [(own * spec[i, 0] + turned * spec[i, 1]).astype(jnp.bfloat16) for i in range(count)],
            axis=1,
        )
        both = dot(wave, product) * (1.0 / side)
        lag = []
        for i in range(count):
            part = both[:, i * LANES : (i + 1) * LANES]
            turned = swap(part[lags:])
            lag.append(part[:lags] + jnp.where(real_lag, -turned, turned))
        lag = jnp.concatenate(lag, axis=1).astype(jnp.bfloat16)
        return dot(lag, over_l[...]).astype(jnp.bfloat16).reshape(tiles, lags // tiles, 2 * lags)

    def cor_copy(s, dt):
        to = lax.rem(t + dt, tiles)
        return pltpu.make_async_remote_copy(
            src_ref=cor_out.at[s, to],
            dst_ref=cor_in.at[s, dt],
            send_sem=cor_send.at[s, dt],
            recv_sem=cor_recv.at[s, dt],
            device_id={"blk": lax.rem(b + blks - s, blks), "tile": to},
            device_id_type=MESH,
        )

    def one(step):
        s = by_distance(step, -1, False) if few else step
        slot = lax.rem(b + blks - s, blks)

        def arrive():
            for h in range(PARTS):
                mic_copy(s, slot, h).wait_recv()

        if line and step == 3:
            pl.when(jnp.logical_not(middle))(arrive)
        else:
            arrive()
        cor_out[s] = correlate(slot)
        for dt in range(tiles):
            cor_copy(s, dt).start()

    cor_out[0] = correlate(b)
    for dt in range(1, tiles):
        cor_copy(0, dt).start()
    cor_in[0, 0] = cor_out[0, t]
    over(1, blks, one)

    for dt in range(1, tiles):
        cor_copy(0, dt).wait_recv()

    def arrived(s):
        for dt in range(tiles):
            cor_copy(s, dt).wait_recv()

    over(1, blks, arrived)
    total = jnp.sum(cor_in[...].astype(jnp.float32), axis=1) * (1.0 / side)
    best = jnp.max(total, axis=0)
    summed = jnp.sum(total, axis=0)
    squares = jnp.sum(total * total, axis=0)
    out[0] = jnp.maximum(best, pltpu.roll(best, lags, 1))[:, :lags]
    out[1] = (summed + pltpu.roll(summed, lags, 1))[:, :lags]
    out[2] = (squares + pltpu.roll(squares, lags, 1))[:, :lags]

    for dt in range(1, tiles):
        g_copy(dt, t).wait_send()
        ctf_copy(dt, t).wait_send()
        cor_copy(0, dt).wait_send()

    def left(s):
        for dt in range(tiles):
            cor_copy(s, dt).wait_send()

    over(1, blks, left)
    for h in range(PARTS):
        to_others(h, lambda c: c.wait_send())
    if line:

        @pl.when(middle)
        def _():
            for h in range(PARTS):
                relay_copy(h).wait_send()


def line_kernel(
    side,
    box,
    lags,
    orient_hbm,
    defocus_hbm,
    piece_hbm,
    bank_hbm,
    ctf_hbm,
    over_n_hbm,
    cs_hbm,
    pick_hbm,
    flip_hbm,
    over_l_hbm,
    out,
    orient,
    defocus,
    piece,
    bank,
    ctf,
    over_n,
    cs,
    pick,
    flip,
    over_l,
    g_out,
    g_in,
    ctf_out,
    ctf_in,
    spec,
    mic,
    cor_out,
    cor_in,
    load_sem,
    g_send,
    own_send,
    pass_send,
    g_recv,
    ctf_send,
    ctf_recv,
    relay_send,
    cor_send,
    cor_recv,
):
    blks = tiles = 4
    b = lax.axis_index("blk")
    t = lax.axis_index("tile")
    pair = t + 1 - 2 * lax.rem(t, 2)
    across = lax.rem(t + 2, tiles)
    order = (t, pair, across, lax.rem(pair + 2, tiles))
    mate = b + 1 - 2 * lax.rem(b, 2)
    near = 2 - b // 2
    far = 3 - 3 * (b // 2)
    middle = jnp.logical_or(b == 1, b == 2)
    count = spec.shape[0]
    chunk = LANES // 2

    def swap(x):
        return pltpu.roll(x, chunk, 1)

    names = ("piece", "over_n", "pick", "defocus", "ctf", "bank", "orient", "cs", "flip", "over_l")
    pairs = (
        (piece_hbm.at[0], piece),
        (over_n_hbm, over_n),
        (pick_hbm, pick),
        (defocus_hbm, defocus),
        (ctf_hbm, ctf),
        (bank_hbm, bank),
        (orient_hbm, orient),
        (cs_hbm, cs),
        (flip_hbm, flip),
        (over_l_hbm.at[t], over_l),
    )
    loads = {
        n: pltpu.make_async_copy(p[0], p[1], load_sem.at[i])
        for i, (n, p) in enumerate(zip(names, pairs))
    }
    for n in names[:2]:
        loads[n].start()

    barrier = pltpu.get_barrier_semaphore()

    def greet(level, tos):
        for to in tos:
            pl.semaphore_signal(
                barrier, inc=1, device_id={"blk": level, "tile": to}, device_id_type=MESH
            )

    greet(b, order[1:])

    @pl.when(middle)
    def _():
        greet(near, order)
        greet(far, order[:2])
        greet(mate, order[:2])

    @pl.when(jnp.logical_not(middle))
    def _():
        greet(mate, order)

    for n in names[2:]:
        loads[n].start()

    loads["piece"].wait()
    loads["over_n"].wait()
    spread_out = dot(piece[...], over_n[...]).astype(jnp.bfloat16)
    for to in range(tiles):
        g_out[to] = spread_out[:, to * LANES : (to + 1) * LANES]

    def g_copy(source, src, sem, level, to):
        return pltpu.make_async_remote_copy(
            src_ref=src,
            dst_ref=g_in.at[b, source],
            send_sem=sem,
            recv_sem=g_recv.at[b, source],
            device_id={"blk": level, "tile": to},
            device_id_type=MESH,
        )

    def g_near(i, k):
        to = order[i]
        return g_copy(t, g_out.at[to], g_send.at[i, k], (near, mate)[k], to)

    def g_own(i):
        to = order[i]
        return g_copy(t, g_out.at[to], own_send.at[i - 1], b, to)

    def g_pass(i, k):
        source = order[i]
        return g_copy(source, g_in.at[b, source], pass_send.at[i - 2, k], (near, mate)[k], t)

    ends = jnp.logical_not(middle)

    def g_sends(act):
        for i in (2, 3):
            act(g_own(i))
        for i in (0, 1):
            act(g_near(i, 0))
            act(g_near(i, 1))

        @pl.when(middle)
        def _():
            for i in (2, 3):
                act(g_near(i, 0))

        @pl.when(middle)
        def _():
            for i in (2, 3):
                act(g_near(i, 1))

        act(g_own(1))

    def passes(i, act):
        pl.when(ends)(lambda: act(g_pass(i, 0)))
        pl.when(ends)(lambda: act(g_pass(i, 1)))

    def arrive(j, i):
        part = g_in.at[j, order[i]]
        pltpu.make_async_remote_copy(
            src_ref=part,
            dst_ref=part,
            send_sem=own_send.at[0],
            recv_sem=g_recv.at[j, order[i]],
            device_id={"blk": mate, "tile": t},
            device_id_type=MESH,
        ).wait_recv()

    def relay_copy(k, i):
        j, source = (near, far)[k], order[i]
        part = g_in.at[j, source]
        return pltpu.make_async_remote_copy(
            src_ref=part,
            dst_ref=part,
            send_sem=relay_send.at[k, i],
            recv_sem=g_recv.at[j, source],
            device_id={"blk": mate, "tile": t},
            device_id_type=MESH,
        )

    def relay(k, blocks):
        inside = middle if blocks[0] < 2 else True
        @pl.when(inside)
        def _():
            for i in blocks:
                copy = relay_copy(k, i)
                copy.wait_recv()
                copy.start()

    lane = lax.broadcasted_iota(jnp.int32, (side, LANES), 1)
    real = lane < chunk
    for n in ("ctf", "pick", "defocus"):
        loads[n].wait()
    for i in range(count):
        taken = dot(ctf[defocus[i]], pick[...]).astype(jnp.bfloat16)
        for to in range(tiles):
            ctf_out[to, i] = taken[:, to * LANES : (to + 1) * LANES]

    def ctf_copy(i, source):
        to = order[i]
        return pltpu.make_async_remote_copy(
            src_ref=ctf_out.at[to],
            dst_ref=ctf_in.at[source],
            send_sem=ctf_send.at[i - 1],
            recv_sem=ctf_recv.at[i - 1],
            device_id={"tile": to},
            device_id_type=MESH,
        )

    pl.semaphore_wait(barrier, jnp.where(middle, 11, 7))
    g_sends(lambda c: c.start())
    g_in[b, t] = g_out[t]
    ctf_in[t] = ctf_out[t]

    loads["bank"].wait()
    loads["orient"].wait()
    columns = over_n[:box, pl.ds(pl.multiple_of(t * LANES, LANES), LANES)]
    firsts = []
    for i in range(count):
        image = bank[orient[i]].astype(jnp.float32)
        centre = jnp.sum(image, keepdims=True) * (1.0 / (box * box))
        image = image - centre
        spread = jnp.sum(image * image, keepdims=True) * (1.0 / (box * box))
        scale = 1.0 / (box * jnp.sqrt(spread + 1e-05))
        template = (image * scale).astype(jnp.bfloat16)
        firsts.append(dot(template, columns).astype(jnp.bfloat16))
        if i == 0:
            for dt in (2, 3, 1):
                ctf_copy(dt, t).start()
    @pl.when(ends)
    def _():
        for i in (2, 3):
            arrive(b, i)
            passes(i, lambda c: c.start())

    loads["cs"].wait()
    tmpl = dot(cs[:, :box], jnp.concatenate(firsts, axis=1))
    relay(0, (0,))
    relay(1, (0,))
    relay(0, (1,))
    relay(1, (1,))

    def transform(j):
        spread_in = g_in[j].reshape(side, LANES)
        turned = swap(dot(cs[side:], spread_in))
        straight = dot(cs[:side], spread_in)
        mic[j] = (straight + jnp.where(real, turned, -turned)).astype(jnp.bfloat16)

    @pl.when(middle)
    def _():
        arrive(b, 2)
        arrive(b, 3)

    arrive(b, 1)
    transform(b)
    def rest(j):
        for i in range(tiles):
            arrive(j, i)

    @pl.when(b == 2)
    def _():
        relay(1, (2, 3))
        relay(0, (2, 3))
        transform(far)
        transform(near)

    @pl.when(b == 1)
    def _():
        relay(0, (2, 3))
        rest(mate)
        transform(mate)

    loads["flip"].wait()
    loads["over_l"].wait()
    for i in (1, 2, 3):
        ctf_copy(i, order[i]).wait_recv()
    for i in range(count):
        here = ctf_in[:, i].reshape(side, LANES)
        gain = here.astype(jnp.float32) + swap(dot(flip[...], here))
        gain = jnp.where(real, gain, swap(gain))
        part = tmpl[:, i * LANES : (i + 1) * LANES]
        turned = swap(part[side:])
        value = (part[:side] + jnp.where(real, turned, -turned)) * gain
        other = swap(value)
        spec[i, 0] = jnp.where(real, value, other)
        spec[i, 1] = jnp.where(real, other, -value)

    wave = jnp.concatenate([cs[:lags], cs[side : side + lags]], axis=0)
    real_lag = lax.broadcasted_iota(jnp.int32, (lags, LANES), 1) < chunk

    def correlate(j):
        own = mic[j].astype(jnp.float32)
        turned = swap(own)
        product = jnp.concatenate(
            [(own * spec[i, 0] + turned * spec[i, 1]).astype(jnp.bfloat16) for i in range(count)],
            axis=1,
        )
        both = dot(wave, product) * (1.0 / side)
        lag = []
        for i in range(count):
            part = both[:, i * LANES : (i + 1) * LANES]
            turned = swap(part[lags:])
            lag.append(part[:lags] + jnp.where(real_lag, -turned, turned))
        lag = jnp.concatenate(lag, axis=1).astype(jnp.bfloat16)
        return dot(lag, over_l[...]).astype(jnp.bfloat16).reshape(tiles, lags // tiles, 2 * lags)

    def cor_copy(s, dt):
        to = lax.rem(t + dt, tiles)
        return pltpu.make_async_remote_copy(
            src_ref=cor_out.at[s, to],
            dst_ref=cor_in.at[s, dt],
            send_sem=cor_send.at[s, dt],
            recv_sem=cor_recv.at[s, dt],
            device_id={"blk": lax.rem(b + blks - s, blks), "tile": to},
            device_id_type=MESH,
        )

    def one(j):
        s = lax.rem(b + blks - j, blks)
        cor_out[s] = correlate(j)
        for dt in range(tiles):
            cor_copy(s, dt).start()

    cor_out[0] = correlate(b)
    for dt in range(1, tiles):
        cor_copy(0, dt).start()
    cor_in[0, 0] = cor_out[0, t]

    @pl.when(b == 1)
    def _():
        relay(1, (2, 3))

    for k, levels in enumerate(((1, 0, 0, 2), (2, 2, 1, 0), (3, 3, 3, 1))):
        j = jnp.where(b < 2, jnp.where(b == 0, levels[0], levels[1]), jnp.where(b == 2, levels[2], levels[3]))
        if k < 2:

            @pl.when(ends)
            def _():
                rest(j)
                transform(j)
        else:
            pl.when(b != 1)(lambda: rest(j))
            transform(j)
        one(j)
        if k == 0:
            @pl.when(b == 1)
            def _():
                transform(near)

    for s in range(blks):
        for dt in range(0 if s else 1, tiles):
            cor_copy(s, dt).wait_recv()
    total = jnp.sum(cor_in[...].astype(jnp.float32), axis=1) * (1.0 / side)
    best = jnp.max(total, axis=0)
    summed = jnp.sum(total, axis=0)
    squares = jnp.sum(total * total, axis=0)
    out[0] = jnp.maximum(best, pltpu.roll(best, lags, 1))[:, :lags]
    out[1] = (summed + pltpu.roll(summed, lags, 1))[:, :lags]
    out[2] = (squares + pltpu.roll(squares, lags, 1))[:, :lags]

    g_sends(lambda c: c.wait_send())
    for i in (1, 2, 3):
        ctf_copy(i, t).wait_send()
    for i in (2, 3):
        passes(i, lambda c: c.wait_send())
    for s in range(blks):
        for dt in range(0 if s else 1, tiles):
            cor_copy(s, dt).wait_send()

    @pl.when(middle)
    def _():
        for k in range(2):
            for i in range(tiles):
                relay_copy(k, i).wait_send()


def on_device(blks, tiles, pieces, bank, orient_ids, defocus_ids, ctf):
    side, box = pieces.shape[2], bank.shape[1]
    rows, lags, count = side // tiles, side - box, orient_ids.shape[0]
    tables = make_tables(side, box, lags, tiles)
    over_n, cs, pick, flip, over_l = tables
    bf16, dma = jnp.bfloat16, pltpu.SemaphoreType.DMA
    hbm_spec = pl.BlockSpec(memory_space=pltpu.HBM)
    line = blks == 4 and tiles == 4
    loaded = [
        pltpu.SMEM(orient_ids.shape, jnp.int32),
        pltpu.SMEM(defocus_ids.shape, jnp.int32),
        pltpu.VMEM((rows, side), bf16),
        pltpu.VMEM(bank.shape, bf16),
        pltpu.VMEM(ctf.shape, bf16),
        pltpu.VMEM(over_n.shape, bf16),
        pltpu.VMEM(cs.shape, bf16),
        pltpu.VMEM(pick.shape, bf16),
        pltpu.VMEM(flip.shape, bf16),
        pltpu.VMEM(over_l.shape[1:], bf16),
    ]
    gain = [pltpu.VMEM((tiles, count, rows, LANES), bf16)] * 2
    spec = pltpu.VMEM((count, 2, side, LANES), jnp.float32)
    cor = [pltpu.VMEM((blks, tiles, lags // tiles, 2 * lags), bf16)] * 2
    if line:
        body = functools.partial(line_kernel, side, box, lags)
        scratch = [
            *loaded,
            pltpu.VMEM((tiles, rows, LANES), bf16),
            pltpu.VMEM((blks, tiles, rows, LANES), bf16),
            *gain,
            spec,
            pltpu.VMEM((blks, side, LANES), bf16),
            *cor,
            dma((10,)),
            dma((4, 2)),
            dma((3,)),
            dma((2, 2)),
            dma((blks, tiles)),
            dma((tiles - 1,)),
            dma((tiles - 1,)),
            dma((2, tiles)),
            dma((blks, tiles)),
            dma((blks, tiles)),
        ]
    else:
        body = functools.partial(kernel, blks, tiles, side, box, lags)
        scratch = [
            *loaded,
            pltpu.VMEM((tiles, rows, LANES), bf16),
            pltpu.VMEM((tiles, rows, LANES), bf16),
            *gain,
            spec,
            pltpu.VMEM((blks, side, LANES), bf16),
            *cor,
            dma((10,)),
            dma((tiles - 1,)),
            dma((tiles - 1,)),
            dma((tiles - 1,)),
            dma((tiles - 1,)),
            dma((blks - 1, PARTS)),
            dma((blks - 1, PARTS)),
            dma((PARTS,)),
            dma((blks, tiles)),
            dma((blks, tiles)),
        ]
    stats = pl.pallas_call(
        body,
        out_shape=pltpu.VMEM((3, lags // tiles, lags), jnp.float32),
        in_specs=[hbm_spec] * 10,
        out_specs=pl.BlockSpec(memory_space=pltpu.VMEM),
        scratch_shapes=scratch,
        compiler_params=pltpu.CompilerParams(
            collective_id=0, has_side_effects=True, vmem_limit_bytes=56 * 2**20
        ),
    )(orient_ids, defocus_ids, pieces, bank, ctf, *tables)
    return stats[0:1], stats[1:2], stats[2:3]


def solution(mesh):
    blks, tiles = mesh.shape["blk"], mesh.shape["tile"]
    placed = (
        P(("grp", "blk"), "tile", None),
        P("blk", None, None),
        P("blk"),
        P(("grp", "blk")),
        P("grp", "tile", None),
    )
    out = P(("grp", "blk"), "tile", None)
    return jax.shard_map(
        functools.partial(on_device, blks, tiles),
        mesh=mesh,
        in_specs=placed,
        out_specs=(out, out, out),
        check_vma=False,
    )
```

```python
import functools
import math

import jax
import jax.numpy as jnp
import ml_dtypes
import numpy as np
from jax import lax
from jax.experimental import pallas as pl
from jax.experimental.pallas import tpu as pltpu
from jax.sharding import PartitionSpec as P

MESH = pl.DeviceIdType.MESH
LANES = 128
PARTS = 2


def make_tables(side, box, lags, tiles):
    half = side // 2
    chunk = LANES // 2
    index = np.arange(side)
    angle = (index[:, None] * index[None, :] % side) * (2.0 * math.pi / side)
    cos, sin = np.cos(angle), np.sin(angle)
    over_n = np.zeros((side, tiles, 2, chunk))
    pick = np.zeros((side, tiles, 2, chunk))
    over_l = np.zeros((tiles, 2, 2, chunk, 2, lags))
    for l in range(half + 1):
        t, c = divmod(l, chunk)
        over_n[:, t, 0, c], over_n[:, t, 1, c] = cos[:, l], -sin[:, l]
        pick[l, t, 0, c] = 1.0
        if 0 < l < half:
            pick[side - l, t, 1, c] = 1.0
        for i in range(2):
            over_l[t, i, 0, c, i] = cos[l, :lags]
            over_l[t, i, 1, c, i] = -sin[l, :lags]
    flip = np.zeros((side, side))
    flip[index, -index % side] = 1.0
    tables = (
        over_n.reshape(side, -1),
        np.concatenate([cos, sin]),
        pick.reshape(side, -1),
        flip,
        over_l.reshape(tiles, 4 * chunk, 2 * lags),
    )
    return [jnp.asarray(m.astype(ml_dtypes.bfloat16)) for m in tables]


def dot(a, b):
    return jnp.dot(a, b, preferred_element_type=jnp.float32)


def kernel(
    blks,
    tiles,
    side,
    box,
    lags,
    orient_hbm,
    defocus_hbm,
    piece_hbm,
    bank_hbm,
    ctf_hbm,
    over_n_hbm,
    cs_hbm,
    pick_hbm,
    flip_hbm,
    over_l_hbm,
    out,
    orient,
    defocus,
    piece,
    bank,
    ctf,
    over_n,
    cs,
    pick,
    flip,
    over_l,
    g_out,
    g_in,
    ctf_out,
    ctf_in,
    spec,
    mic,
    cor_out,
    cor_in,
    load_sem,
    g_send,
    g_recv,
    ctf_send,
    ctf_recv,
    mic_send,
    mic_recv,
    relay_send,
    cor_send,
    cor_recv,
):
    b = lax.axis_index("blk")
    t = lax.axis_index("tile")
    rows = side // tiles
    count = spec.shape[0]
    chunk = LANES // 2
    few = blks <= 8
    line = blks == 4
    middle = jnp.logical_or(b == 1, b == 2)
    piece_rows = side // PARTS

    def over(start, stop, body):
        if few:
            for s in range(start, stop):
                body(s)
        else:

            @pl.loop(start, stop)
            def _(s):
                body(s)

    def by_distance(step, sign, far):
        offset = None
        for me in range(blks):
            others = [j for j in range(blks) if j != me]
            others.sort(key=lambda j: abs(j - me), reverse=far)
            value = jnp.int32(sign * (others[step - 1] - me) % blks)
            offset = value if me == 0 else jnp.where(b == me, value, offset)
        return offset

    def swap(x):
        return pltpu.roll(x, chunk, 1)

    names = ("piece", "over_n", "cs", "ctf", "pick", "defocus", "bank", "orient", "flip", "over_l")
    pairs = (
        (piece_hbm.at[0], piece),
        (over_n_hbm, over_n),
        (cs_hbm, cs),
        (ctf_hbm, ctf),
        (pick_hbm, pick),
        (defocus_hbm, defocus),
        (bank_hbm, bank),
        (orient_hbm, orient),
        (flip_hbm, flip),
        (over_l_hbm.at[t], over_l),
    )
    loads = {
        n: pltpu.make_async_copy(p[0], p[1], load_sem.at[i])
        for i, (n, p) in enumerate(zip(names, pairs))
    }
    for n in names[:2]:
        loads[n].start()

    barrier = pltpu.get_barrier_semaphore()
    for dt in range(1, tiles):
        pl.semaphore_signal(
            barrier, inc=1, device_id={"tile": lax.rem(t + dt, tiles)}, device_id_type=MESH
        )

    def greet(s):
        pl.semaphore_signal(
            barrier, inc=1, device_id={"blk": lax.rem(b + s, blks)}, device_id_type=MESH
        )

    over(1, blks, greet)
    for n in names[2:]:
        loads[n].start()

    loads["piece"].wait()
    loads["over_n"].wait()
    spread_out = dot(piece[...], over_n[...]).astype(jnp.bfloat16)
    for to in range(tiles):
        g_out[to] = spread_out[:, to * LANES : (to + 1) * LANES]

    def g_copy(dt, source):
        to = lax.rem(t + dt, tiles)
        return pltpu.make_async_remote_copy(
            src_ref=g_out.at[to],
            dst_ref=g_in.at[source],
            send_sem=g_send.at[dt - 1],
            recv_sem=g_recv.at[dt - 1],
            device_id={"tile": to},
            device_id_type=MESH,
        )

    pl.semaphore_wait(barrier, tiles + blks - 2)
    for dt in range(1, tiles):
        g_copy(dt, t).start()
    g_in[t] = g_out[t]

    loads["cs"].wait()
    for dt in range(1, tiles):
        g_copy(dt, lax.rem(t + tiles - dt, tiles)).wait_recv()
    lane = lax.broadcasted_iota(jnp.int32, (side, LANES), 1)
    real = lane < chunk
    spread_in = g_in[...].reshape(side, LANES)

    def mic_copy(s, slot, h):
        part = mic.at[slot, pl.ds(h * piece_rows, piece_rows)]
        return pltpu.make_async_remote_copy(
            src_ref=part,
            dst_ref=part,
            send_sem=mic_send.at[s - 1, h],
            recv_sem=mic_recv.at[s - 1, h],
            device_id={"blk": lax.rem(b + s, blks)},
            device_id_type=MESH,
        )

    def relay_copy(h):
        part = mic.at[lax.rem(b + 2, blks), pl.ds(h * piece_rows, piece_rows)]
        return pltpu.make_async_remote_copy(
            src_ref=part,
            dst_ref=part,
            send_sem=relay_send.at[h],
            recv_sem=mic_recv.at[jnp.where(b == 2, 2, 0), h],
            device_id={"blk": jnp.where(b == 2, 3, 0)},
            device_id_type=MESH,
        )

    def relay(h):
        if line:

            @pl.when(middle)
            def _():
                mic_copy(2, lax.rem(b + 2, blks), h).wait_recv()
                relay_copy(h).start()

    def to_others(h, act):
        def one_of(s):
            if line and s == 1:

                @pl.when(middle)
                def _():
                    act(mic_copy(by_distance(s, 1, True), b, h))

            else:
                act(mic_copy(by_distance(s, 1, True) if few else s, b, h))

        over(1, blks, one_of)

    for h in range(PARTS):
        low, high = h * piece_rows, (h + 1) * piece_rows
        turned = swap(dot(cs[side + low : side + high], spread_in))
        straight = dot(cs[low:high], spread_in)
        mic[b, low:high] = (straight + jnp.where(real[:piece_rows], turned, -turned)).astype(
            jnp.bfloat16
        )
        to_others(h, lambda c: c.start())

    for n in ("ctf", "pick", "defocus"):
        loads[n].wait()
    for i in range(count):
        taken = dot(ctf[defocus[i]], pick[...]).astype(jnp.bfloat16)
        for to in range(tiles):
            ctf_out[to, i] = taken[:, to * LANES : (to + 1) * LANES]

    def ctf_copy(dt, source):
        to = lax.rem(t + dt, tiles)
        return pltpu.make_async_remote_copy(
            src_ref=ctf_out.at[to],
            dst_ref=ctf_in.at[source],
            send_sem=ctf_send.at[dt - 1],
            recv_sem=ctf_recv.at[dt - 1],
            device_id={"tile": to},
            device_id_type=MESH,
        )

    for dt in range(1, tiles):
        ctf_copy(dt, t).start()
    ctf_in[t] = ctf_out[t]

    loads["bank"].wait()
    loads["orient"].wait()
    columns = over_n[:box, pl.ds(pl.multiple_of(t * LANES, LANES), LANES)]
    firsts = []
    for i in range(count):
        image = bank[orient[i]].astype(jnp.float32)
        centre = jnp.sum(image, keepdims=True) * (1.0 / (box * box))
        image = image - centre
        spread = jnp.sum(image * image, keepdims=True) * (1.0 / (box * box))
        scale = 1.0 / (box * jnp.sqrt(spread + 1e-05))
        template = (image * scale).astype(jnp.bfloat16)
        firsts.append(dot(template, columns).astype(jnp.bfloat16))
    relay(0)
    tmpl = dot(cs[:, :box], jnp.concatenate(firsts, axis=1))

    loads["flip"].wait()
    loads["over_l"].wait()
    for dt in range(1, tiles):
        ctf_copy(dt, lax.rem(t + tiles - dt, tiles)).wait_recv()
    for i in range(count):
        here = ctf_in[:, i].reshape(side, LANES)
        gain = here.astype(jnp.float32) + swap(dot(flip[...], here))
        gain = jnp.where(real, gain, swap(gain))
        part = tmpl[:, i * LANES : (i + 1) * LANES]
        turned = swap(part[side:])
        value = (part[:side] + jnp.where(real, turned, -turned)) * gain
        other = swap(value)
        spec[i, 0] = jnp.where(real, value, other)
        spec[i, 1] = jnp.where(real, other, -value)

    for h in range(1, PARTS):
        relay(h)
    wave = jnp.concatenate([cs[:lags], cs[side : side + lags]], axis=0)
    real_lag = lax.broadcasted_iota(jnp.int32, (lags, LANES), 1) < chunk

    def correlate(slot):
        own = mic[slot].astype(jnp.float32)
        turned = swap(own)
        product = jnp.concatenate(
            [(own * spec[i, 0] + turned * spec[i, 1]).astype(jnp.bfloat16) for i in range(count)],
            axis=1,
        )
        both = dot(wave, product) * (1.0 / side)
        lag = []
        for i in range(count):
            part = both[:, i * LANES : (i + 1) * LANES]
            turned = swap(part[lags:])
            lag.append(part[:lags] + jnp.where(real_lag, -turned, turned))
        lag = jnp.concatenate(lag, axis=1).astype(jnp.bfloat16)
        return dot(lag, over_l[...]).astype(jnp.bfloat16).reshape(tiles, lags // tiles, 2 * lags)

    def cor_copy(s, dt):
        to = lax.rem(t + dt, tiles)
        return pltpu.make_async_remote_copy(
            src_ref=cor_out.at[s, to],
            dst_ref=cor_in.at[s, dt],
            send_sem=cor_send.at[s, dt],
            recv_sem=cor_recv.at[s, dt],
            device_id={"blk": lax.rem(b + blks - s, blks), "tile": to},
            device_id_type=MESH,
        )

    def one(step):
        s = by_distance(step, -1, False) if few else step
        slot = lax.rem(b + blks - s, blks)

        def arrive():
            for h in range(PARTS):
                mic_copy(s, slot, h).wait_recv()

        if line and step == 3:
            pl.when(jnp.logical_not(middle))(arrive)
        else:
            arrive()
        cor_out[s] = correlate(slot)
        for dt in range(tiles):
            cor_copy(s, dt).start()

    cor_out[0] = correlate(b)
    for dt in range(1, tiles):
        cor_copy(0, dt).start()
    cor_in[0, 0] = cor_out[0, t]
    over(1, blks, one)

    for dt in range(1, tiles):
        cor_copy(0, dt).wait_recv()

    def arrived(s):
        for dt in range(tiles):
            cor_copy(s, dt).wait_recv()

    over(1, blks, arrived)
    total = jnp.sum(cor_in[...].astype(jnp.float32), axis=1) * (1.0 / side)
    best = jnp.max(total, axis=0)
    summed = jnp.sum(total, axis=0)
    squares = jnp.sum(total * total, axis=0)
    out[0] = jnp.maximum(best, pltpu.roll(best, lags, 1))[:, :lags]
    out[1] = (summed + pltpu.roll(summed, lags, 1))[:, :lags]
    out[2] = (squares + pltpu.roll(squares, lags, 1))[:, :lags]

    for dt in range(1, tiles):
        g_copy(dt, t).wait_send()
        ctf_copy(dt, t).wait_send()
        cor_copy(0, dt).wait_send()

    def left(s):
        for dt in range(tiles):
            cor_copy(s, dt).wait_send()

    over(1, blks, left)
    for h in range(PARTS):
        to_others(h, lambda c: c.wait_send())
    if line:

        @pl.when(middle)
        def _():
            for h in range(PARTS):
                relay_copy(h).wait_send()


def line_kernel(
    side,
    box,
    lags,
    orient_hbm,
    defocus_hbm,
    piece_hbm,
    bank_hbm,
    ctf_hbm,
    over_n_hbm,
    cs_hbm,
    pick_hbm,
    flip_hbm,
    over_l_hbm,
    out,
    orient,
    defocus,
    piece,
    bank,
    ctf,
    over_n,
    cs,
    pick,
    flip,
    over_l,
    g_out,
    g_in,
    ctf_out,
    ctf_in,
    spec,
    mic,
    cor_out,
    cor_in,
    load_sem,
    g_send,
    own_send,
    pass_send,
    g_recv,
    ctf_send,
    ctf_recv,
    relay_send,
    cor_send,
    cor_recv,
):
    blks = tiles = 4
    b = lax.axis_index("blk")
    t = lax.axis_index("tile")
    pair = t + 1 - 2 * lax.rem(t, 2)
    across = lax.rem(t + 2, tiles)
    order = (t, pair, across, lax.rem(pair + 2, tiles))
    mate = b + 1 - 2 * lax.rem(b, 2)
    near = 2 - b // 2
    far = 3 - 3 * (b // 2)
    middle = jnp.logical_or(b == 1, b == 2)
    count = spec.shape[0]
    chunk = LANES // 2

    def swap(x):
        return pltpu.roll(x, chunk, 1)

    names = ("piece", "over_n", "pick", "defocus", "ctf", "bank", "orient", "cs", "flip", "over_l")
    pairs = (
        (piece_hbm.at[0], piece),
        (over_n_hbm, over_n),
        (pick_hbm, pick),
        (defocus_hbm, defocus),
        (ctf_hbm, ctf),
        (bank_hbm, bank),
        (orient_hbm, orient),
        (cs_hbm, cs),
        (flip_hbm, flip),
        (over_l_hbm.at[t], over_l),
    )
    loads = {
        n: pltpu.make_async_copy(p[0], p[1], load_sem.at[i])
        for i, (n, p) in enumerate(zip(names, pairs))
    }
    for n in names[:2]:
        loads[n].start()

    barrier = pltpu.get_barrier_semaphore()

    def greet(level, tos):
        for to in tos:
            pl.semaphore_signal(
                barrier, inc=1, device_id={"blk": level, "tile": to}, device_id_type=MESH
            )

    greet(b, order[1:])

    @pl.when(middle)
    def _():
        greet(near, order)
        greet(far, order[:2])
        greet(mate, order[:2])

    @pl.when(jnp.logical_not(middle))
    def _():
        greet(far, order[:1])
        greet(mate, order)

    for n in names[2:]:
        loads[n].start()

    loads["piece"].wait()
    loads["over_n"].wait()
    spread_out = dot(piece[...], over_n[...]).astype(jnp.bfloat16)
    for to in range(tiles):
        g_out[to] = spread_out[:, to * LANES : (to + 1) * LANES]

    def g_copy(source, src, sem, level, to):
        return pltpu.make_async_remote_copy(
            src_ref=src,
            dst_ref=g_in.at[b, source],
            send_sem=sem,
            recv_sem=g_recv.at[b, source],
            device_id={"blk": level, "tile": to},
            device_id_type=MESH,
        )

    def g_near(i, k):
        to = order[i]
        return g_copy(t, g_out.at[to], g_send.at[i, k], (near, mate)[k], to)

    def g_own(i):
        to = order[i]
        return g_copy(t, g_out.at[to], own_send.at[i - 1], b, to)

    def g_pass(i, k):
        source = order[i]
        return g_copy(source, g_in.at[b, source], pass_send.at[i - 2, k], (far, near, mate)[k], t)

    ends = jnp.logical_not(middle)

    def g_sends(act):
        for i in (2, 3):
            act(g_own(i))
        for i in (0, 1):
            act(g_near(i, 0))
            act(g_near(i, 1))

        @pl.when(middle)
        def _():
            for i in (2, 3):
                act(g_near(i, 0))

        @pl.when(middle)
        def _():
            for i in (2, 3):
                act(g_near(i, 1))

        act(g_own(1))

    def passes(act):
        for k in range(3):
            for i in (2, 3):
                act(g_pass(i, k))

    def arrive(j, i):
        part = g_in.at[j, order[i]]
        pltpu.make_async_remote_copy(
            src_ref=part,
            dst_ref=part,
            send_sem=own_send.at[0],
            recv_sem=g_recv.at[j, order[i]],
            device_id={"blk": mate, "tile": t},
            device_id_type=MESH,
        ).wait_recv()

    def relay_copy(k, i):
        j, source = (near, far)[k], order[i]
        part = g_in.at[j, source]
        return pltpu.make_async_remote_copy(
            src_ref=part,
            dst_ref=part,
            send_sem=relay_send.at[k, i],
            recv_sem=g_recv.at[j, source],
            device_id={"blk": mate, "tile": t},
            device_id_type=MESH,
        )

    def relay(k, blocks):
        inside = middle if blocks[0] < 2 else True
        @pl.when(inside)
        def _():
            for i in blocks:
                copy = relay_copy(k, i)
                copy.wait_recv()
                copy.start()

    lane = lax.broadcasted_iota(jnp.int32, (side, LANES), 1)
    real = lane < chunk
    for n in ("ctf", "pick", "defocus"):
        loads[n].wait()
    for i in range(count):
        taken = dot(ctf[defocus[i]], pick[...]).astype(jnp.bfloat16)
        for to in range(tiles):
            ctf_out[to, i] = taken[:, to * LANES : (to + 1) * LANES]

    def ctf_copy(i, source):
        to = order[i]
        return pltpu.make_async_remote_copy(
            src_ref=ctf_out.at[to],
            dst_ref=ctf_in.at[source],
            send_sem=ctf_send.at[i - 1],
            recv_sem=ctf_recv.at[i - 1],
            device_id={"tile": to},
            device_id_type=MESH,
        )

    pl.semaphore_wait(barrier, jnp.where(middle, 11, 8))
    g_sends(lambda c: c.start())
    g_in[b, t] = g_out[t]
    ctf_in[t] = ctf_out[t]

    loads["bank"].wait()
    loads["orient"].wait()
    columns = over_n[:box, pl.ds(pl.multiple_of(t * LANES, LANES), LANES)]
    firsts = []
    for i in range(count):
        image = bank[orient[i]].astype(jnp.float32)
        centre = jnp.sum(image, keepdims=True) * (1.0 / (box * box))
        image = image - centre
        spread = jnp.sum(image * image, keepdims=True) * (1.0 / (box * box))
        scale = 1.0 / (box * jnp.sqrt(spread + 1e-05))
        template = (image * scale).astype(jnp.bfloat16)
        firsts.append(dot(template, columns).astype(jnp.bfloat16))
        if i == 0:
            for dt in (2, 3, 1):
                ctf_copy(dt, t).start()
    @pl.when(ends)
    def _():
        for i in (2, 3):
            arrive(b, i)
            g_pass(i, 0).start()
        for k in (1, 2):
            for i in (2, 3):
                g_pass(i, k).start()

    loads["cs"].wait()
    tmpl = dot(cs[:, :box], jnp.concatenate(firsts, axis=1))
    relay(0, (0,))
    relay(1, (0,))
    relay(0, (1,))
    relay(1, (1,))

    def transform(j):
        spread_in = g_in[j].reshape(side, LANES)
        turned = swap(dot(cs[side:], spread_in))
        straight = dot(cs[:side], spread_in)
        mic[j] = (straight + jnp.where(real, turned, -turned)).astype(jnp.bfloat16)

    @pl.when(middle)
    def _():
        arrive(b, 2)
        arrive(b, 3)

    arrive(b, 1)
    transform(b)
    def rest(j):
        for i in range(tiles):
            arrive(j, i)

    @pl.when(b == 2)
    def _():
        relay(0, (2, 3))
        transform(near)

    @pl.when(b == 1)
    def _():
        relay(0, (2, 3))
        transform(near)

    loads["flip"].wait()
    loads["over_l"].wait()
    for i in (1, 2, 3):
        ctf_copy(i, order[i]).wait_recv()
    for i in range(count):
        here = ctf_in[:, i].reshape(side, LANES)
        gain = here.astype(jnp.float32) + swap(dot(flip[...], here))
        gain = jnp.where(real, gain, swap(gain))
        part = tmpl[:, i * LANES : (i + 1) * LANES]
        turned = swap(part[side:])
        value = (part[:side] + jnp.where(real, turned, -turned)) * gain
        other = swap(value)
        spec[i, 0] = jnp.where(real, value, other)
        spec[i, 1] = jnp.where(real, other, -value)

    wave = jnp.concatenate([cs[:lags], cs[side : side + lags]], axis=0)
    real_lag = lax.broadcasted_iota(jnp.int32, (lags, LANES), 1) < chunk

    def correlate(j):
        own = mic[j].astype(jnp.float32)
        turned = swap(own)
        product = jnp.concatenate(
            [(own * spec[i, 0] + turned * spec[i, 1]).astype(jnp.bfloat16) for i in range(count)],
            axis=1,
        )
        both = dot(wave, product) * (1.0 / side)
        lag = []
        for i in range(count):
            part = both[:, i * LANES : (i + 1) * LANES]
            turned = swap(part[lags:])
            lag.append(part[:lags] + jnp.where(real_lag, -turned, turned))
        lag = jnp.concatenate(lag, axis=1).astype(jnp.bfloat16)
        return dot(lag, over_l[...]).astype(jnp.bfloat16).reshape(tiles, lags // tiles, 2 * lags)

    def cor_copy(s, dt):
        to = lax.rem(t + dt, tiles)
        return pltpu.make_async_remote_copy(
            src_ref=cor_out.at[s, to],
            dst_ref=cor_in.at[s, dt],
            send_sem=cor_send.at[s, dt],
            recv_sem=cor_recv.at[s, dt],
            device_id={"blk": lax.rem(b + blks - s, blks), "tile": to},
            device_id_type=MESH,
        )

    def one(j):
        s = lax.rem(b + blks - j, blks)
        cor_out[s] = correlate(j)
        for dt in range(tiles):
            cor_copy(s, dt).start()

    cor_out[0] = correlate(b)
    for dt in range(1, tiles):
        cor_copy(0, dt).start()
    cor_in[0, 0] = cor_out[0, t]

    for k, levels in enumerate(((1, 2, 0, 2), (2, 0, 1, 0), (3, 3, 3, 1))):
        j = jnp.where(b < 2, jnp.where(b == 0, levels[0], levels[1]), jnp.where(b == 2, levels[2], levels[3]))
        if k == 0:

            @pl.when(b == 2)
            def _():
                arrive(j, 2)
                arrive(j, 3)

            pl.when(ends)(lambda: rest(j))
            pl.when(b != 1)(lambda: transform(j))
        elif k == 1:

            @pl.when(b != 2)
            def _():
                rest(j)
                transform(j)
        else:

            @pl.when(b == 1)
            def _():
                arrive(j, 2)
                arrive(j, 3)

            pl.when(b != 1)(lambda: rest(j))
            transform(j)
        one(j)
    for s in range(blks):
        for dt in range(0 if s else 1, tiles):
            cor_copy(s, dt).wait_recv()
    total = jnp.sum(cor_in[...].astype(jnp.float32), axis=1) * (1.0 / side)
    best = jnp.max(total, axis=0)
    summed = jnp.sum(total, axis=0)
    squares = jnp.sum(total * total, axis=0)
    out[0] = jnp.maximum(best, pltpu.roll(best, lags, 1))[:, :lags]
    out[1] = (summed + pltpu.roll(summed, lags, 1))[:, :lags]
    out[2] = (squares + pltpu.roll(squares, lags, 1))[:, :lags]

    g_sends(lambda c: c.wait_send())
    for i in (1, 2, 3):
        ctf_copy(i, t).wait_send()
    pl.when(ends)(lambda: passes(lambda c: c.wait_send()))
    for s in range(blks):
        for dt in range(0 if s else 1, tiles):
            cor_copy(s, dt).wait_send()

    @pl.when(middle)
    def _():
        for k in range(2):
            for i in range(tiles if k == 0 else 2):
                relay_copy(k, i).wait_send()


def on_device(blks, tiles, pieces, bank, orient_ids, defocus_ids, ctf):
    side, box = pieces.shape[2], bank.shape[1]
    rows, lags, count = side // tiles, side - box, orient_ids.shape[0]
    tables = make_tables(side, box, lags, tiles)
    over_n, cs, pick, flip, over_l = tables
    bf16, dma = jnp.bfloat16, pltpu.SemaphoreType.DMA
    hbm_spec = pl.BlockSpec(memory_space=pltpu.HBM)
    line = blks == 4 and tiles == 4
    loaded = [
        pltpu.SMEM(orient_ids.shape, jnp.int32),
        pltpu.SMEM(defocus_ids.shape, jnp.int32),
        pltpu.VMEM((rows, side), bf16),
        pltpu.VMEM(bank.shape, bf16),
        pltpu.VMEM(ctf.shape, bf16),
        pltpu.VMEM(over_n.shape, bf16),
        pltpu.VMEM(cs.shape, bf16),
        pltpu.VMEM(pick.shape, bf16),
        pltpu.VMEM(flip.shape, bf16),
        pltpu.VMEM(over_l.shape[1:], bf16),
    ]
    gain = [pltpu.VMEM((tiles, count, rows, LANES), bf16)] * 2
    spec = pltpu.VMEM((count, 2, side, LANES), jnp.float32)
    cor = [pltpu.VMEM((blks, tiles, lags // tiles, 2 * lags), bf16)] * 2
    if line:
        body = functools.partial(line_kernel, side, box, lags)
        scratch = [
            *loaded,
            pltpu.VMEM((tiles, rows, LANES), bf16),
            pltpu.VMEM((blks, tiles, rows, LANES), bf16),
            *gain,
            spec,
            pltpu.VMEM((blks, side, LANES), bf16),
            *cor,
            dma((10,)),
            dma((4, 2)),
            dma((3,)),
            dma((2, 3)),
            dma((blks, tiles)),
            dma((tiles - 1,)),
            dma((tiles - 1,)),
            dma((2, tiles)),
            dma((blks, tiles)),
            dma((blks, tiles)),
        ]
    else:
        body = functools.partial(kernel, blks, tiles, side, box, lags)
        scratch = [
            *loaded,
            pltpu.VMEM((tiles, rows, LANES), bf16),
            pltpu.VMEM((tiles, rows, LANES), bf16),
            *gain,
            spec,
            pltpu.VMEM((blks, side, LANES), bf16),
            *cor,
            dma((10,)),
            dma((tiles - 1,)),
            dma((tiles - 1,)),
            dma((tiles - 1,)),
            dma((tiles - 1,)),
            dma((blks - 1, PARTS)),
            dma((blks - 1, PARTS)),
            dma((PARTS,)),
            dma((blks, tiles)),
            dma((blks, tiles)),
        ]
    stats = pl.pallas_call(
        body,
        out_shape=pltpu.VMEM((3, lags // tiles, lags), jnp.float32),
        in_specs=[hbm_spec] * 10,
        out_specs=pl.BlockSpec(memory_space=pltpu.VMEM),
        scratch_shapes=scratch,
        compiler_params=pltpu.CompilerParams(
            collective_id=0, has_side_effects=True, vmem_limit_bytes=56 * 2**20
        ),
    )(orient_ids, defocus_ids, pieces, bank, ctf, *tables)
    return stats[0:1], stats[1:2], stats[2:3]


def solution(mesh):
    blks, tiles = mesh.shape["blk"], mesh.shape["tile"]
    placed = (
        P(("grp", "blk"), "tile", None),
        P("blk", None, None),
        P("blk"),
        P(("grp", "blk")),
        P("grp", "tile", None),
    )
    out = P(("grp", "blk"), "tile", None)
    return jax.shard_map(
        functools.partial(on_device, blks, tiles),
        mesh=mesh,
        in_specs=placed,
        out_specs=(out, out, out),
        check_vma=False,
    )
```

```python
import functools
import math

import jax
import jax.numpy as jnp
import ml_dtypes
import numpy as np
from jax import lax
from jax.experimental import pallas as pl
from jax.experimental.pallas import tpu as pltpu
from jax.sharding import PartitionSpec as P

MESH = pl.DeviceIdType.MESH
LANES = 128
PARTS = 2


def make_tables(side, box, lags, tiles):
    half = side // 2
    chunk = LANES // 2
    index = np.arange(side)
    angle = (index[:, None] * index[None, :] % side) * (2.0 * math.pi / side)
    cos, sin = np.cos(angle), np.sin(angle)
    over_n = np.zeros((side, tiles, 2, chunk))
    pick = np.zeros((side, tiles, 2, chunk))
    over_l = np.zeros((tiles, 2, 2, chunk, 2, lags))
    for l in range(half + 1):
        t, c = divmod(l, chunk)
        over_n[:, t, 0, c], over_n[:, t, 1, c] = cos[:, l], -sin[:, l]
        pick[l, t, 0, c] = 1.0
        if 0 < l < half:
            pick[side - l, t, 1, c] = 1.0
        for i in range(2):
            over_l[t, i, 0, c, i] = cos[l, :lags]
            over_l[t, i, 1, c, i] = -sin[l, :lags]
    flip = np.zeros((side, side))
    flip[index, -index % side] = 1.0
    tables = (
        over_n.reshape(side, -1),
        np.concatenate([cos, sin]),
        pick.reshape(side, -1),
        flip,
        over_l.reshape(tiles, 4 * chunk, 2 * lags),
    )
    return [jnp.asarray(m.astype(ml_dtypes.bfloat16)) for m in tables]


def dot(a, b):
    return jnp.dot(a, b, preferred_element_type=jnp.float32)


def kernel(
    blks,
    tiles,
    side,
    box,
    lags,
    orient_hbm,
    defocus_hbm,
    piece_hbm,
    bank_hbm,
    ctf_hbm,
    over_n_hbm,
    cs_hbm,
    pick_hbm,
    flip_hbm,
    over_l_hbm,
    out,
    orient,
    defocus,
    piece,
    bank,
    ctf,
    over_n,
    cs,
    pick,
    flip,
    over_l,
    g_out,
    g_in,
    ctf_out,
    ctf_in,
    spec,
    mic,
    cor_out,
    cor_in,
    load_sem,
    g_send,
    g_recv,
    ctf_send,
    ctf_recv,
    mic_send,
    mic_recv,
    relay_send,
    cor_send,
    cor_recv,
):
    b = lax.axis_index("blk")
    t = lax.axis_index("tile")
    rows = side // tiles
    count = spec.shape[0]
    chunk = LANES // 2
    few = blks <= 8
    line = blks == 4
    middle = jnp.logical_or(b == 1, b == 2)
    piece_rows = side // PARTS

    def over(start, stop, body):
        if few:
            for s in range(start, stop):
                body(s)
        else:

            @pl.loop(start, stop)
            def _(s):
                body(s)

    def by_distance(step, sign, far):
        offset = None
        for me in range(blks):
            others = [j for j in range(blks) if j != me]
            others.sort(key=lambda j: abs(j - me), reverse=far)
            value = jnp.int32(sign * (others[step - 1] - me) % blks)
            offset = value if me == 0 else jnp.where(b == me, value, offset)
        return offset

    def swap(x):
        return pltpu.roll(x, chunk, 1)

    names = ("piece", "over_n", "cs", "ctf", "pick", "defocus", "bank", "orient", "flip", "over_l")
    pairs = (
        (piece_hbm.at[0], piece),
        (over_n_hbm, over_n),
        (cs_hbm, cs),
        (ctf_hbm, ctf),
        (pick_hbm, pick),
        (defocus_hbm, defocus),
        (bank_hbm, bank),
        (orient_hbm, orient),
        (flip_hbm, flip),
        (over_l_hbm.at[t], over_l),
    )
    loads = {
        n: pltpu.make_async_copy(p[0], p[1], load_sem.at[i])
        for i, (n, p) in enumerate(zip(names, pairs))
    }
    for n in names[:2]:
        loads[n].start()

    barrier = pltpu.get_barrier_semaphore()
    for dt in range(1, tiles):
        pl.semaphore_signal(
            barrier, inc=1, device_id={"tile": lax.rem(t + dt, tiles)}, device_id_type=MESH
        )

    def greet(s):
        pl.semaphore_signal(
            barrier, inc=1, device_id={"blk": lax.rem(b + s, blks)}, device_id_type=MESH
        )

    over(1, blks, greet)
    for n in names[2:]:
        loads[n].start()

    loads["piece"].wait()
    loads["over_n"].wait()
    spread_out = dot(piece[...], over_n[...]).astype(jnp.bfloat16)
    for to in range(tiles):
        g_out[to] = spread_out[:, to * LANES : (to + 1) * LANES]

    def g_copy(dt, source):
        to = lax.rem(t + dt, tiles)
        return pltpu.make_async_remote_copy(
            src_ref=g_out.at[to],
            dst_ref=g_in.at[source],
            send_sem=g_send.at[dt - 1],
            recv_sem=g_recv.at[dt - 1],
            device_id={"tile": to},
            device_id_type=MESH,
        )

    pl.semaphore_wait(barrier, tiles + blks - 2)
    for dt in range(1, tiles):
        g_copy(dt, t).start()
    g_in[t] = g_out[t]

    loads["cs"].wait()
    for dt in range(1, tiles):
        g_copy(dt, lax.rem(t + tiles - dt, tiles)).wait_recv()
    lane = lax.broadcasted_iota(jnp.int32, (side, LANES), 1)
    real = lane < chunk
    spread_in = g_in[...].reshape(side, LANES)

    def mic_copy(s, slot, h):
        part = mic.at[slot, pl.ds(h * piece_rows, piece_rows)]
        return pltpu.make_async_remote_copy(
            src_ref=part,
            dst_ref=part,
            send_sem=mic_send.at[s - 1, h],
            recv_sem=mic_recv.at[s - 1, h],
            device_id={"blk": lax.rem(b + s, blks)},
            device_id_type=MESH,
        )

    def relay_copy(h):
        part = mic.at[lax.rem(b + 2, blks), pl.ds(h * piece_rows, piece_rows)]
        return pltpu.make_async_remote_copy(
            src_ref=part,
            dst_ref=part,
            send_sem=relay_send.at[h],
            recv_sem=mic_recv.at[jnp.where(b == 2, 2, 0), h],
            device_id={"blk": jnp.where(b == 2, 3, 0)},
            device_id_type=MESH,
        )

    def relay(h):
        if line:

            @pl.when(middle)
            def _():
                mic_copy(2, lax.rem(b + 2, blks), h).wait_recv()
                relay_copy(h).start()

    def to_others(h, act):
        def one_of(s):
            if line and s == 1:

                @pl.when(middle)
                def _():
                    act(mic_copy(by_distance(s, 1, True), b, h))

            else:
                act(mic_copy(by_distance(s, 1, True) if few else s, b, h))

        over(1, blks, one_of)

    for h in range(PARTS):
        low, high = h * piece_rows, (h + 1) * piece_rows
        turned = swap(dot(cs[side + low : side + high], spread_in))
        straight = dot(cs[low:high], spread_in)
        mic[b, low:high] = (straight + jnp.where(real[:piece_rows], turned, -turned)).astype(
            jnp.bfloat16
        )
        to_others(h, lambda c: c.start())

    for n in ("ctf", "pick", "defocus"):
        loads[n].wait()
    for i in range(count):
        taken = dot(ctf[defocus[i]], pick[...]).astype(jnp.bfloat16)
        for to in range(tiles):
            ctf_out[to, i] = taken[:, to * LANES : (to + 1) * LANES]

    def ctf_copy(dt, source):
        to = lax.rem(t + dt, tiles)
        return pltpu.make_async_remote_copy(
            src_ref=ctf_out.at[to],
            dst_ref=ctf_in.at[source],
            send_sem=ctf_send.at[dt - 1],
            recv_sem=ctf_recv.at[dt - 1],
            device_id={"tile": to},
            device_id_type=MESH,
        )

    for dt in range(1, tiles):
        ctf_copy(dt, t).start()
    ctf_in[t] = ctf_out[t]

    loads["bank"].wait()
    loads["orient"].wait()
    columns = over_n[:box, pl.ds(pl.multiple_of(t * LANES, LANES), LANES)]
    firsts = []
    for i in range(count):
        image = bank[orient[i]].astype(jnp.float32)
        centre = jnp.sum(image, keepdims=True) * (1.0 / (box * box))
        image = image - centre
        spread = jnp.sum(image * image, keepdims=True) * (1.0 / (box * box))
        scale = 1.0 / (box * jnp.sqrt(spread + 1e-05))
        template = (image * scale).astype(jnp.bfloat16)
        firsts.append(dot(template, columns).astype(jnp.bfloat16))
    relay(0)
    tmpl = dot(cs[:, :box], jnp.concatenate(firsts, axis=1))

    loads["flip"].wait()
    loads["over_l"].wait()
    for dt in range(1, tiles):
        ctf_copy(dt, lax.rem(t + tiles - dt, tiles)).wait_recv()
    for i in range(count):
        here = ctf_in[:, i].reshape(side, LANES)
        gain = here.astype(jnp.float32) + swap(dot(flip[...], here))
        gain = jnp.where(real, gain, swap(gain))
        part = tmpl[:, i * LANES : (i + 1) * LANES]
        turned = swap(part[side:])
        value = (part[:side] + jnp.where(real, turned, -turned)) * gain
        other = swap(value)
        spec[i, 0] = jnp.where(real, value, other)
        spec[i, 1] = jnp.where(real, other, -value)

    for h in range(1, PARTS):
        relay(h)
    wave = jnp.concatenate([cs[:lags], cs[side : side + lags]], axis=0)
    real_lag = lax.broadcasted_iota(jnp.int32, (lags, LANES), 1) < chunk

    def correlate(slot):
        own = mic[slot].astype(jnp.float32)
        turned = swap(own)
        product = jnp.concatenate(
            [(own * spec[i, 0] + turned * spec[i, 1]).astype(jnp.bfloat16) for i in range(count)],
            axis=1,
        )
        both = dot(wave, product) * (1.0 / side)
        lag = []
        for i in range(count):
            part = both[:, i * LANES : (i + 1) * LANES]
            turned = swap(part[lags:])
            lag.append(part[:lags] + jnp.where(real_lag, -turned, turned))
        lag = jnp.concatenate(lag, axis=1).astype(jnp.bfloat16)
        return dot(lag, over_l[...]).astype(jnp.bfloat16).reshape(tiles, lags // tiles, 2 * lags)

    def cor_copy(s, dt):
        to = lax.rem(t + dt, tiles)
        return pltpu.make_async_remote_copy(
            src_ref=cor_out.at[s, to],
            dst_ref=cor_in.at[s, dt],
            send_sem=cor_send.at[s, dt],
            recv_sem=cor_recv.at[s, dt],
            device_id={"blk": lax.rem(b + blks - s, blks), "tile": to},
            device_id_type=MESH,
        )

    def one(step):
        s = by_distance(step, -1, False) if few else step
        slot = lax.rem(b + blks - s, blks)

        def arrive():
            for h in range(PARTS):
                mic_copy(s, slot, h).wait_recv()

        if line and step == 3:
            pl.when(jnp.logical_not(middle))(arrive)
        else:
            arrive()
        cor_out[s] = correlate(slot)
        for dt in range(tiles):
            cor_copy(s, dt).start()

    cor_out[0] = correlate(b)
    for dt in range(1, tiles):
        cor_copy(0, dt).start()
    cor_in[0, 0] = cor_out[0, t]
    over(1, blks, one)

    for dt in range(1, tiles):
        cor_copy(0, dt).wait_recv()

    def arrived(s):
        for dt in range(tiles):
            cor_copy(s, dt).wait_recv()

    over(1, blks, arrived)
    total = jnp.sum(cor_in[...].astype(jnp.float32), axis=1) * (1.0 / side)
    best = jnp.max(total, axis=0)
    summed = jnp.sum(total, axis=0)
    squares = jnp.sum(total * total, axis=0)
    out[0] = jnp.maximum(best, pltpu.roll(best, lags, 1))[:, :lags]
    out[1] = (summed + pltpu.roll(summed, lags, 1))[:, :lags]
    out[2] = (squares + pltpu.roll(squares, lags, 1))[:, :lags]

    for dt in range(1, tiles):
        g_copy(dt, t).wait_send()
        ctf_copy(dt, t).wait_send()
        cor_copy(0, dt).wait_send()

    def left(s):
        for dt in range(tiles):
            cor_copy(s, dt).wait_send()

    over(1, blks, left)
    for h in range(PARTS):
        to_others(h, lambda c: c.wait_send())
    if line:

        @pl.when(middle)
        def _():
            for h in range(PARTS):
                relay_copy(h).wait_send()


def line_kernel(
    side,
    box,
    lags,
    orient_hbm,
    defocus_hbm,
    piece_hbm,
    bank_hbm,
    ctf_hbm,
    over_n_hbm,
    cs_hbm,
    pick_hbm,
    flip_hbm,
    over_l_hbm,
    out,
    orient,
    defocus,
    piece,
    bank,
    ctf,
    over_n,
    cs,
    pick,
    flip,
    over_l,
    g_out,
    g_in,
    ctf_out,
    ctf_in,
    spec,
    mic,
    cor_out,
    cor_in,
    load_sem,
    g_send,
    g_recv,
    ctf_sem,
    cor_send,
    cor_recv,
):
    blks = tiles = 4
    b = lax.axis_index("blk")
    t = lax.axis_index("tile")
    pair = t + 1 - 2 * lax.rem(t, 2)
    across = lax.rem(t + 2, tiles)
    order = (t, pair, across, lax.rem(pair + 2, tiles))
    mate = b + 1 - 2 * lax.rem(b, 2)
    near = 2 - b // 2
    far = 3 - 3 * (b // 2)
    middle = jnp.logical_or(b == 1, b == 2)
    count = spec.shape[0]
    chunk = LANES // 2

    def swap(x):
        return pltpu.roll(x, chunk, 1)

    names = ("piece", "over_n", "pick", "defocus", "ctf", "bank", "orient", "cs", "flip", "over_l")
    pairs = (
        (piece_hbm.at[0], piece),
        (over_n_hbm, over_n),
        (pick_hbm, pick),
        (defocus_hbm, defocus),
        (ctf_hbm, ctf),
        (bank_hbm, bank),
        (orient_hbm, orient),
        (cs_hbm, cs),
        (flip_hbm, flip),
        (over_l_hbm.at[t], over_l),
    )
    loads = {
        n: pltpu.make_async_copy(p[0], p[1], load_sem.at[i])
        for i, (n, p) in enumerate(zip(names, pairs))
    }
    for n in names[:2]:
        loads[n].start()

    def drain(part, sem):
        pltpu.make_async_copy(part, part, sem).wait()

    barrier = pltpu.get_barrier_semaphore()

    def greet(level, tos):
        for to in tos:
            pl.semaphore_signal(
                barrier, inc=1, device_id={"blk": level, "tile": to}, device_id_type=MESH
            )

    greet(b, order[1:])

    @pl.when(middle)
    def _():
        greet(near, order)
        greet(far, order[:2])
        greet(mate, order[:2])

    @pl.when(jnp.logical_not(middle))
    def _():
        greet(far, order[:1])
        greet(mate, order)

    for n in names[2:]:
        loads[n].start()

    loads["piece"].wait()
    loads["over_n"].wait()
    spread_out = dot(piece[...], over_n[...]).astype(jnp.bfloat16)
    for to in range(tiles):
        g_out[to] = spread_out[:, to * LANES : (to + 1) * LANES]

    def g_copy(source, src, sem, level, to):
        return pltpu.make_async_remote_copy(
            src_ref=src,
            dst_ref=g_in.at[b, source],
            send_sem=sem,
            recv_sem=g_recv.at[b, source],
            device_id={"blk": level, "tile": to},
            device_id_type=MESH,
        )

    def g_near(i, k):
        to = order[i]
        return g_copy(t, g_out.at[to], g_send.at[0], (near, mate)[k], to)

    def g_own(i):
        to = order[i]
        return g_copy(t, g_out.at[to], g_send.at[1], b, to)

    def g_pass(i, k):
        source = order[i]
        return g_copy(source, g_in.at[b, source], g_send.at[2], (far, near, mate)[k], t)

    ends = jnp.logical_not(middle)

    def g_sends(act):
        for i in (2, 3):
            act(g_own(i))
        for i in (0, 1):
            act(g_near(i, 0))
            act(g_near(i, 1))

        @pl.when(middle)
        def _():
            for i in (2, 3):
                act(g_near(i, 0))

        @pl.when(middle)
        def _():
            for i in (2, 3):
                act(g_near(i, 1))

        act(g_own(1))

    def passes(act):
        for k in range(3):
            for i in (2, 3):
                act(g_pass(i, k))

    def arrive(j, i):
        part = g_in.at[j, order[i]]
        pltpu.make_async_remote_copy(
            src_ref=part,
            dst_ref=part,
            send_sem=g_send.at[0],
            recv_sem=g_recv.at[j, order[i]],
            device_id={"blk": mate, "tile": t},
            device_id_type=MESH,
        ).wait_recv()

    def relay_copy(k, i):
        j, source = (near, far)[k], order[i]
        part = g_in.at[j, source]
        return pltpu.make_async_remote_copy(
            src_ref=part,
            dst_ref=part,
            send_sem=g_send.at[2],
            recv_sem=g_recv.at[j, source],
            device_id={"blk": mate, "tile": t},
            device_id_type=MESH,
        )

    def relay(k, blocks):
        inside = middle if blocks[0] < 2 else True
        @pl.when(inside)
        def _():
            for i in blocks:
                copy = relay_copy(k, i)
                copy.wait_recv()
                copy.start()

    lane = lax.broadcasted_iota(jnp.int32, (side, LANES), 1)
    real = lane < chunk
    for n in ("ctf", "pick", "defocus"):
        loads[n].wait()
    for i in range(count):
        taken = dot(ctf[defocus[i]], pick[...]).astype(jnp.bfloat16)
        for to in range(tiles):
            ctf_out[to, i] = taken[:, to * LANES : (to + 1) * LANES]

    def ctf_copy(i, source):
        to = order[i]
        return pltpu.make_async_remote_copy(
            src_ref=ctf_out.at[to],
            dst_ref=ctf_in.at[source],
            send_sem=ctf_sem.at[0],
            recv_sem=ctf_sem.at[1],
            device_id={"tile": to},
            device_id_type=MESH,
        )

    pl.semaphore_wait(barrier, jnp.where(middle, 11, 8))
    g_sends(lambda c: c.start())
    g_in[b, t] = g_out[t]
    ctf_in[t] = ctf_out[t]

    loads["bank"].wait()
    loads["orient"].wait()
    columns = over_n[:box, pl.ds(pl.multiple_of(t * LANES, LANES), LANES)]
    firsts = []
    for i in range(count):
        image = bank[orient[i]].astype(jnp.float32)
        centre = jnp.sum(image, keepdims=True) * (1.0 / (box * box))
        image = image - centre
        spread = jnp.sum(image * image, keepdims=True) * (1.0 / (box * box))
        scale = 1.0 / (box * jnp.sqrt(spread + 1e-05))
        template = (image * scale).astype(jnp.bfloat16)
        firsts.append(dot(template, columns).astype(jnp.bfloat16))
        if i == 0:
            for dt in (2, 3, 1):
                ctf_copy(dt, t).start()
    @pl.when(ends)
    def _():
        for i in (2, 3):
            arrive(b, i)
            g_pass(i, 0).start()
        for k in (1, 2):
            for i in (2, 3):
                g_pass(i, k).start()

    loads["cs"].wait()
    tmpl = dot(cs[:, :box], jnp.concatenate(firsts, axis=1))
    relay(0, (0,))
    relay(1, (0,))
    relay(0, (1,))
    relay(1, (1,))

    def transform(j):
        spread_in = g_in[j].reshape(side, LANES)
        turned = swap(dot(cs[side:], spread_in))
        straight = dot(cs[:side], spread_in)
        mic[j] = (straight + jnp.where(real, turned, -turned)).astype(jnp.bfloat16)

    @pl.when(middle)
    def _():
        arrive(b, 2)
        arrive(b, 3)

    arrive(b, 1)
    transform(b)
    def rest(j):
        for i in range(tiles):
            arrive(j, i)

    @pl.when(b == 2)
    def _():
        relay(0, (2, 3))
        transform(near)

    @pl.when(b == 1)
    def _():
        relay(0, (2, 3))
        transform(near)

    loads["flip"].wait()
    loads["over_l"].wait()
    drain(ctf_in.at[: tiles - 1], ctf_sem.at[1])
    for i in range(count):
        here = ctf_in[:, i].reshape(side, LANES)
        gain = here.astype(jnp.float32) + swap(dot(flip[...], here))
        gain = jnp.where(real, gain, swap(gain))
        part = tmpl[:, i * LANES : (i + 1) * LANES]
        turned = swap(part[side:])
        value = (part[:side] + jnp.where(real, turned, -turned)) * gain
        other = swap(value)
        spec[i, 0] = jnp.where(real, value, other)
        spec[i, 1] = jnp.where(real, other, -value)

    wave = jnp.concatenate([cs[:lags], cs[side : side + lags]], axis=0)
    real_lag = lax.broadcasted_iota(jnp.int32, (lags, LANES), 1) < chunk

    def correlate(j):
        own = mic[j].astype(jnp.float32)
        turned = swap(own)
        product = jnp.concatenate(
            [(own * spec[i, 0] + turned * spec[i, 1]).astype(jnp.bfloat16) for i in range(count)],
            axis=1,
        )
        both = dot(wave, product) * (1.0 / side)
        lag = []
        for i in range(count):
            part = both[:, i * LANES : (i + 1) * LANES]
            turned = swap(part[lags:])
            lag.append(part[:lags] + jnp.where(real_lag, -turned, turned))
        lag = jnp.concatenate(lag, axis=1).astype(jnp.bfloat16)
        return dot(lag, over_l[...]).astype(jnp.bfloat16).reshape(tiles, lags // tiles, 2 * lags)

    def cor_copy(s, dt, kind):
        to = lax.rem(t + dt, tiles)
        return pltpu.make_async_remote_copy(
            src_ref=cor_out.at[s, to],
            dst_ref=cor_in.at[s, dt],
            send_sem=cor_send.at[kind],
            recv_sem=cor_recv.at[kind],
            device_id={"blk": lax.rem(b + blks - s, blks), "tile": to},
            device_id_type=MESH,
        )

    def one(j):
        s = lax.rem(b + blks - j, blks)
        cor_out[s] = correlate(j)
        for dt in range(tiles):
            cor_copy(s, dt, 1).start()

    cor_out[0] = correlate(b)
    for dt in range(1, tiles):
        cor_copy(0, dt, 0).start()
    cor_in[0, 0] = cor_out[0, t]

    for k, levels in enumerate(((1, 2, 0, 2), (3, 0, 1, 0), (2, 3, 3, 1))):
        j = jnp.where(b < 2, jnp.where(b == 0, levels[0], levels[1]), jnp.where(b == 2, levels[2], levels[3]))
        if k == 0:

            @pl.when(b == 2)
            def _():
                arrive(j, 2)
                arrive(j, 3)

            pl.when(ends)(lambda: rest(j))
            pl.when(b != 1)(lambda: transform(j))
        elif k == 1:

            @pl.when(b != 2)
            def _():
                rest(j)
                transform(j)
        else:

            @pl.when(b == 1)
            def _():
                arrive(j, 2)
                arrive(j, 3)

            pl.when(b != 1)(lambda: rest(j))
            transform(j)
        one(j)
    drain(cor_in.at[0, 1:], cor_recv.at[0])
    drain(cor_in.at[1:], cor_recv.at[1])
    total = jnp.sum(cor_in[...].astype(jnp.float32), axis=1) * (1.0 / side)
    best = jnp.max(total, axis=0)
    summed = jnp.sum(total, axis=0)
    squares = jnp.sum(total * total, axis=0)
    out[0] = jnp.maximum(best, pltpu.roll(best, lags, 1))[:, :lags]
    out[1] = (summed + pltpu.roll(summed, lags, 1))[:, :lags]
    out[2] = (squares + pltpu.roll(squares, lags, 1))[:, :lags]

    drain(g_in.at[0, 1:], g_send.at[1])
    drain(g_in.at[1:, :2], g_send.at[2])
    drain(ctf_out.at[: tiles - 1], ctf_sem.at[0])
    drain(cor_out.at[0, 1:], cor_send.at[0])
    drain(cor_out.at[1:], cor_send.at[1])
    pl.when(middle)(lambda: drain(g_in.at[:2], g_send.at[0]))
    pl.when(ends)(lambda: drain(g_in.at[0], g_send.at[0]))


def on_device(blks, tiles, pieces, bank, orient_ids, defocus_ids, ctf):
    side, box = pieces.shape[2], bank.shape[1]
    rows, lags, count = side // tiles, side - box, orient_ids.shape[0]
    tables = make_tables(side, box, lags, tiles)
    over_n, cs, pick, flip, over_l = tables
    bf16, dma = jnp.bfloat16, pltpu.SemaphoreType.DMA
    hbm_spec = pl.BlockSpec(memory_space=pltpu.HBM)
    line = blks == 4 and tiles == 4
    loaded = [
        pltpu.SMEM(orient_ids.shape, jnp.int32),
        pltpu.SMEM(defocus_ids.shape, jnp.int32),
        pltpu.VMEM((rows, side), bf16),
        pltpu.VMEM(bank.shape, bf16),
        pltpu.VMEM(ctf.shape, bf16),
        pltpu.VMEM(over_n.shape, bf16),
        pltpu.VMEM(cs.shape, bf16),
        pltpu.VMEM(pick.shape, bf16),
        pltpu.VMEM(flip.shape, bf16),
        pltpu.VMEM(over_l.shape[1:], bf16),
    ]
    gain = [pltpu.VMEM((tiles, count, rows, LANES), bf16)] * 2
    spec = pltpu.VMEM((count, 2, side, LANES), jnp.float32)
    cor = [pltpu.VMEM((blks, tiles, lags // tiles, 2 * lags), bf16)] * 2
    if line:
        body = functools.partial(line_kernel, side, box, lags)
        scratch = [
            *loaded,
            pltpu.VMEM((tiles, rows, LANES), bf16),
            pltpu.VMEM((blks, tiles, rows, LANES), bf16),
            *gain,
            spec,
            pltpu.VMEM((blks, side, LANES), bf16),
            *cor,
            dma((10,)),
            dma((3,)),
            dma((blks, tiles)),
            dma((2,)),
            dma((2,)),
            dma((2,)),
        ]
    else:
        body = functools.partial(kernel, blks, tiles, side, box, lags)
        scratch = [
            *loaded,
            pltpu.VMEM((tiles, rows, LANES), bf16),
            pltpu.VMEM((tiles, rows, LANES), bf16),
            *gain,
            spec,
            pltpu.VMEM((blks, side, LANES), bf16),
            *cor,
            dma((10,)),
            dma((tiles - 1,)),
            dma((tiles - 1,)),
            dma((tiles - 1,)),
            dma((tiles - 1,)),
            dma((blks - 1, PARTS)),
            dma((blks - 1, PARTS)),
            dma((PARTS,)),
            dma((blks, tiles)),
            dma((blks, tiles)),
        ]
    stats = pl.pallas_call(
        body,
        out_shape=pltpu.VMEM((3, lags // tiles, lags), jnp.float32),
        in_specs=[hbm_spec] * 10,
        out_specs=pl.BlockSpec(memory_space=pltpu.VMEM),
        scratch_shapes=scratch,
        compiler_params=pltpu.CompilerParams(
            collective_id=0, has_side_effects=True, vmem_limit_bytes=56 * 2**20
        ),
    )(orient_ids, defocus_ids, pieces, bank, ctf, *tables)
    return stats[0:1], stats[1:2], stats[2:3]


def solution(mesh):
    blks, tiles = mesh.shape["blk"], mesh.shape["tile"]
    placed = (
        P(("grp", "blk"), "tile", None),
        P("blk", None, None),
        P("blk"),
        P(("grp", "blk")),
        P("grp", "tile", None),
    )
    out = P(("grp", "blk"), "tile", None)
    return jax.shard_map(
        functools.partial(on_device, blks, tiles),
        mesh=mesh,
        in_specs=placed,
        out_specs=(out, out, out),
        check_vma=False,
    )
```

```python
import functools
import math

import jax
import jax.numpy as jnp
import ml_dtypes
import numpy as np
from jax import lax
from jax.experimental import pallas as pl
from jax.experimental.pallas import tpu as pltpu
from jax.sharding import PartitionSpec as P

MESH = pl.DeviceIdType.MESH
LANES = 128
PARTS = 2


def make_tables(side, box, lags, tiles):
    half = side // 2
    chunk = LANES // 2
    index = np.arange(side)
    angle = (index[:, None] * index[None, :] % side) * (2.0 * math.pi / side)
    cos, sin = np.cos(angle), np.sin(angle)
    over_n = np.zeros((side, tiles, 2, chunk))
    pick = np.zeros((side, tiles, 2, chunk))
    over_l = np.zeros((tiles, 2, 2, chunk, 2, lags))
    for l in range(half + 1):
        t, c = divmod(l, chunk)
        over_n[:, t, 0, c], over_n[:, t, 1, c] = cos[:, l], -sin[:, l]
        pick[l, t, 0, c] = 1.0
        if 0 < l < half:
            pick[side - l, t, 1, c] = 1.0
        for i in range(2):
            over_l[t, i, 0, c, i] = cos[l, :lags]
            over_l[t, i, 1, c, i] = -sin[l, :lags]
    flip = np.zeros((side, side))
    flip[index, -index % side] = 1.0
    tables = (
        over_n.reshape(side, -1),
        np.concatenate([cos, sin]),
        pick.reshape(side, -1),
        flip,
        over_l.reshape(tiles, 4 * chunk, 2 * lags),
    )
    return [jnp.asarray(m.astype(ml_dtypes.bfloat16)) for m in tables]


def dot(a, b):
    return jnp.dot(a, b, preferred_element_type=jnp.float32)


def kernel(
    blks,
    tiles,
    side,
    box,
    lags,
    orient_hbm,
    defocus_hbm,
    piece_hbm,
    bank_hbm,
    ctf_hbm,
    over_n_hbm,
    cs_hbm,
    pick_hbm,
    flip_hbm,
    over_l_hbm,
    out,
    orient,
    defocus,
    piece,
    bank,
    ctf,
    over_n,
    cs,
    pick,
    flip,
    over_l,
    g_out,
    g_in,
    ctf_out,
    ctf_in,
    spec,
    mic,
    cor_out,
    cor_in,
    load_sem,
    g_send,
    g_recv,
    ctf_send,
    ctf_recv,
    mic_send,
    mic_recv,
    relay_send,
    cor_send,
    cor_recv,
):
    b = lax.axis_index("blk")
    t = lax.axis_index("tile")
    rows = side // tiles
    count = spec.shape[0]
    chunk = LANES // 2
    few = blks <= 8
    line = blks == 4
    middle = jnp.logical_or(b == 1, b == 2)
    piece_rows = side // PARTS

    def over(start, stop, body):
        if few:
            for s in range(start, stop):
                body(s)
        else:

            @pl.loop(start, stop)
            def _(s):
                body(s)

    def by_distance(step, sign, far):
        offset = None
        for me in range(blks):
            others = [j for j in range(blks) if j != me]
            others.sort(key=lambda j: abs(j - me), reverse=far)
            value = jnp.int32(sign * (others[step - 1] - me) % blks)
            offset = value if me == 0 else jnp.where(b == me, value, offset)
        return offset

    def swap(x):
        return pltpu.roll(x, chunk, 1)

    names = ("piece", "over_n", "cs", "ctf", "pick", "defocus", "bank", "orient", "flip", "over_l")
    pairs = (
        (piece_hbm.at[0], piece),
        (over_n_hbm, over_n),
        (cs_hbm, cs),
        (ctf_hbm, ctf),
        (pick_hbm, pick),
        (defocus_hbm, defocus),
        (bank_hbm, bank),
        (orient_hbm, orient),
        (flip_hbm, flip),
        (over_l_hbm.at[t], over_l),
    )
    loads = {
        n: pltpu.make_async_copy(p[0], p[1], load_sem.at[i])
        for i, (n, p) in enumerate(zip(names, pairs))
    }
    for n in names[:2]:
        loads[n].start()

    barrier = pltpu.get_barrier_semaphore()
    for dt in range(1, tiles):
        pl.semaphore_signal(
            barrier, inc=1, device_id={"tile": lax.rem(t + dt, tiles)}, device_id_type=MESH
        )

    def greet(s):
        pl.semaphore_signal(
            barrier, inc=1, device_id={"blk": lax.rem(b + s, blks)}, device_id_type=MESH
        )

    over(1, blks, greet)
    for n in names[2:]:
        loads[n].start()

    loads["piece"].wait()
    loads["over_n"].wait()
    spread_out = dot(piece[...], over_n[...]).astype(jnp.bfloat16)
    for to in range(tiles):
        g_out[to] = spread_out[:, to * LANES : (to + 1) * LANES]

    def g_copy(dt, source):
        to = lax.rem(t + dt, tiles)
        return pltpu.make_async_remote_copy(
            src_ref=g_out.at[to],
            dst_ref=g_in.at[source],
            send_sem=g_send.at[dt - 1],
            recv_sem=g_recv.at[dt - 1],
            device_id={"tile": to},
            device_id_type=MESH,
        )

    pl.semaphore_wait(barrier, tiles + blks - 2)
    for dt in range(1, tiles):
        g_copy(dt, t).start()
    g_in[t] = g_out[t]

    loads["cs"].wait()
    for dt in range(1, tiles):
        g_copy(dt, lax.rem(t + tiles - dt, tiles)).wait_recv()
    lane = lax.broadcasted_iota(jnp.int32, (side, LANES), 1)
    real = lane < chunk
    spread_in = g_in[...].reshape(side, LANES)

    def mic_copy(s, slot, h):
        part = mic.at[slot, pl.ds(h * piece_rows, piece_rows)]
        return pltpu.make_async_remote_copy(
            src_ref=part,
            dst_ref=part,
            send_sem=mic_send.at[s - 1, h],
            recv_sem=mic_recv.at[s - 1, h],
            device_id={"blk": lax.rem(b + s, blks)},
            device_id_type=MESH,
        )

    def relay_copy(h):
        part = mic.at[lax.rem(b + 2, blks), pl.ds(h * piece_rows, piece_rows)]
        return pltpu.make_async_remote_copy(
            src_ref=part,
            dst_ref=part,
            send_sem=relay_send.at[h],
            recv_sem=mic_recv.at[jnp.where(b == 2, 2, 0), h],
            device_id={"blk": jnp.where(b == 2, 3, 0)},
            device_id_type=MESH,
        )

    def relay(h):
        if line:

            @pl.when(middle)
            def _():
                mic_copy(2, lax.rem(b + 2, blks), h).wait_recv()
                relay_copy(h).start()

    def to_others(h, act):
        def one_of(s):
            if line and s == 1:

                @pl.when(middle)
                def _():
                    act(mic_copy(by_distance(s, 1, True), b, h))

            else:
                act(mic_copy(by_distance(s, 1, True) if few else s, b, h))

        over(1, blks, one_of)

    for h in range(PARTS):
        low, high = h * piece_rows, (h + 1) * piece_rows
        turned = swap(dot(cs[side + low : side + high], spread_in))
        straight = dot(cs[low:high], spread_in)
        mic[b, low:high] = (straight + jnp.where(real[:piece_rows], turned, -turned)).astype(
            jnp.bfloat16
        )
        to_others(h, lambda c: c.start())

    for n in ("ctf", "pick", "defocus"):
        loads[n].wait()
    for i in range(count):
        taken = dot(ctf[defocus[i]], pick[...]).astype(jnp.bfloat16)
        for to in range(tiles):
            ctf_out[to, i] = taken[:, to * LANES : (to + 1) * LANES]

    def ctf_copy(dt, source):
        to = lax.rem(t + dt, tiles)
        return pltpu.make_async_remote_copy(
            src_ref=ctf_out.at[to],
            dst_ref=ctf_in.at[source],
            send_sem=ctf_send.at[dt - 1],
            recv_sem=ctf_recv.at[dt - 1],
            device_id={"tile": to},
            device_id_type=MESH,
        )

    for dt in range(1, tiles):
        ctf_copy(dt, t).start()
    ctf_in[t] = ctf_out[t]

    loads["bank"].wait()
    loads["orient"].wait()
    columns = over_n[:box, pl.ds(pl.multiple_of(t * LANES, LANES), LANES)]
    firsts = []
    for i in range(count):
        image = bank[orient[i]].astype(jnp.float32)
        centre = jnp.sum(image, keepdims=True) * (1.0 / (box * box))
        image = image - centre
        spread = jnp.sum(image * image, keepdims=True) * (1.0 / (box * box))
        scale = 1.0 / (box * jnp.sqrt(spread + 1e-05))
        template = (image * scale).astype(jnp.bfloat16)
        firsts.append(dot(template, columns).astype(jnp.bfloat16))
    relay(0)
    tmpl = dot(cs[:, :box], jnp.concatenate(firsts, axis=1))

    loads["flip"].wait()
    loads["over_l"].wait()
    for dt in range(1, tiles):
        ctf_copy(dt, lax.rem(t + tiles - dt, tiles)).wait_recv()
    for i in range(count):
        here = ctf_in[:, i].reshape(side, LANES)
        gain = here.astype(jnp.float32) + swap(dot(flip[...], here))
        gain = jnp.where(real, gain, swap(gain))
        part = tmpl[:, i * LANES : (i + 1) * LANES]
        turned = swap(part[side:])
        value = (part[:side] + jnp.where(real, turned, -turned)) * gain
        other = swap(value)
        spec[i, 0] = jnp.where(real, value, other)
        spec[i, 1] = jnp.where(real, other, -value)

    for h in range(1, PARTS):
        relay(h)
    wave = jnp.concatenate([cs[:lags], cs[side : side + lags]], axis=0)
    real_lag = lax.broadcasted_iota(jnp.int32, (lags, LANES), 1) < chunk

    def correlate(slot):
        own = mic[slot].astype(jnp.float32)
        turned = swap(own)
        product = jnp.concatenate(
            [(own * spec[i, 0] + turned * spec[i, 1]).astype(jnp.bfloat16) for i in range(count)],
            axis=1,
        )
        both = dot(wave, product) * (1.0 / side)
        lag = []
        for i in range(count):
            part = both[:, i * LANES : (i + 1) * LANES]
            turned = swap(part[lags:])
            lag.append(part[:lags] + jnp.where(real_lag, -turned, turned))
        lag = jnp.concatenate(lag, axis=1).astype(jnp.bfloat16)
        return dot(lag, over_l[...]).astype(jnp.bfloat16).reshape(tiles, lags // tiles, 2 * lags)

    def cor_copy(s, dt):
        to = lax.rem(t + dt, tiles)
        return pltpu.make_async_remote_copy(
            src_ref=cor_out.at[s, to],
            dst_ref=cor_in.at[s, dt],
            send_sem=cor_send.at[s, dt],
            recv_sem=cor_recv.at[s, dt],
            device_id={"blk": lax.rem(b + blks - s, blks), "tile": to},
            device_id_type=MESH,
        )

    def one(step):
        s = by_distance(step, -1, False) if few else step
        slot = lax.rem(b + blks - s, blks)

        def arrive():
            for h in range(PARTS):
                mic_copy(s, slot, h).wait_recv()

        if line and step == 3:
            pl.when(jnp.logical_not(middle))(arrive)
        else:
            arrive()
        cor_out[s] = correlate(slot)
        for dt in range(tiles):
            cor_copy(s, dt).start()

    cor_out[0] = correlate(b)
    for dt in range(1, tiles):
        cor_copy(0, dt).start()
    cor_in[0, 0] = cor_out[0, t]
    over(1, blks, one)

    for dt in range(1, tiles):
        cor_copy(0, dt).wait_recv()

    def arrived(s):
        for dt in range(tiles):
            cor_copy(s, dt).wait_recv()

    over(1, blks, arrived)
    total = jnp.sum(cor_in[...].astype(jnp.float32), axis=1) * (1.0 / side)
    best = jnp.max(total, axis=0)
    summed = jnp.sum(total, axis=0)
    squares = jnp.sum(total * total, axis=0)
    out[0] = jnp.maximum(best, pltpu.roll(best, lags, 1))[:, :lags]
    out[1] = (summed + pltpu.roll(summed, lags, 1))[:, :lags]
    out[2] = (squares + pltpu.roll(squares, lags, 1))[:, :lags]

    for dt in range(1, tiles):
        g_copy(dt, t).wait_send()
        ctf_copy(dt, t).wait_send()
        cor_copy(0, dt).wait_send()

    def left(s):
        for dt in range(tiles):
            cor_copy(s, dt).wait_send()

    over(1, blks, left)
    for h in range(PARTS):
        to_others(h, lambda c: c.wait_send())
    if line:

        @pl.when(middle)
        def _():
            for h in range(PARTS):
                relay_copy(h).wait_send()


def line_kernel(
    side,
    box,
    lags,
    orient_hbm,
    defocus_hbm,
    piece_hbm,
    bank_hbm,
    ctf_hbm,
    over_n_hbm,
    cs_hbm,
    pick_hbm,
    flip_hbm,
    over_l_hbm,
    out,
    orient,
    defocus,
    piece,
    bank,
    ctf,
    over_n,
    cs,
    pick,
    flip,
    over_l,
    g_out,
    g_in,
    ctf_out,
    ctf_in,
    spec,
    mic,
    cor_out,
    cor_in,
    load_sem,
    g_send,
    g_recv,
    ctf_sem,
    cor_send,
    cor_recv,
):
    blks = tiles = 4
    b = lax.axis_index("blk")
    t = lax.axis_index("tile")
    pair = t + 1 - 2 * lax.rem(t, 2)
    across = lax.rem(t + 2, tiles)
    order = (t, pair, across, lax.rem(pair + 2, tiles))
    mate = b + 1 - 2 * lax.rem(b, 2)
    near = 2 - b // 2
    far = 3 - 3 * (b // 2)
    middle = jnp.logical_or(b == 1, b == 2)
    count = spec.shape[0]
    chunk = LANES // 2

    def swap(x):
        return pltpu.roll(x, chunk, 1)

    names = ("piece", "over_n", "pick", "defocus", "ctf", "bank", "orient", "cs", "flip", "over_l")
    pairs = (
        (piece_hbm.at[0], piece),
        (over_n_hbm, over_n),
        (pick_hbm, pick),
        (defocus_hbm, defocus),
        (ctf_hbm, ctf),
        (bank_hbm, bank),
        (orient_hbm, orient),
        (cs_hbm, cs),
        (flip_hbm, flip),
        (over_l_hbm.at[t], over_l),
    )
    loads = {
        n: pltpu.make_async_copy(p[0], p[1], load_sem.at[i])
        for i, (n, p) in enumerate(zip(names, pairs))
    }
    for n in names[:2]:
        loads[n].start()

    def drain(part, sem):
        pltpu.make_async_copy(part, part, sem).wait()

    barrier = pltpu.get_barrier_semaphore()

    def greet(level, tos):
        for to in tos:
            pl.semaphore_signal(
                barrier, inc=1, device_id={"blk": level, "tile": to}, device_id_type=MESH
            )

    greet(b, order[1:])

    @pl.when(middle)
    def _():
        greet(near, order)
        greet(far, order[:2])
        greet(mate, order[:2])

    @pl.when(b == 1)
    def _():
        greet(mate, order[2:])

    @pl.when(jnp.logical_not(middle))
    def _():
        greet(far, order[:1])
        greet(mate, order)

    for n in names[2:]:
        loads[n].start()

    loads["piece"].wait()
    loads["over_n"].wait()
    spread_out = dot(piece[...], over_n[...]).astype(jnp.bfloat16)
    for to in range(tiles):
        g_out[to] = spread_out[:, to * LANES : (to + 1) * LANES]

    def g_copy(source, src, sem, level, to):
        return pltpu.make_async_remote_copy(
            src_ref=src,
            dst_ref=g_in.at[b, source],
            send_sem=sem,
            recv_sem=g_recv.at[b, source],
            device_id={"blk": level, "tile": to},
            device_id_type=MESH,
        )

    def g_near(i, k):
        to = order[i]
        return g_copy(t, g_out.at[to], g_send.at[0], (near, mate)[k], to)

    def g_own(i):
        to = order[i]
        return g_copy(t, g_out.at[to], g_send.at[1], b, to)

    def g_pass(i, k):
        source = order[i]
        return g_copy(source, g_in.at[b, source], g_send.at[2], (far, near, mate)[k], t)

    ends = jnp.logical_not(middle)

    def g_sends(act):
        for i in (2, 3):
            act(g_own(i))
        for i in (0, 1):
            act(g_near(i, 0))
            act(g_near(i, 1))

        @pl.when(middle)
        def _():
            for i in (2, 3):
                act(g_near(i, 0))

        @pl.when(b < 3)
        def _():
            for i in (2, 3):
                act(g_near(i, 1))

        act(g_own(1))

    def passes(act):
        for k in range(3):
            for i in (2, 3):
                act(g_pass(i, k))

    def arrive(j, i):
        part = g_in.at[j, order[i]]
        pltpu.make_async_remote_copy(
            src_ref=part,
            dst_ref=part,
            send_sem=g_send.at[0],
            recv_sem=g_recv.at[j, order[i]],
            device_id={"blk": mate, "tile": t},
            device_id_type=MESH,
        ).wait_recv()

    def relay_copy(k, i):
        j, source = (near, far)[k], order[i]
        part = g_in.at[j, source]
        return pltpu.make_async_remote_copy(
            src_ref=part,
            dst_ref=part,
            send_sem=g_send.at[2],
            recv_sem=g_recv.at[j, source],
            device_id={"blk": mate, "tile": t},
            device_id_type=MESH,
        )

    def relay(k, blocks):
        inside = middle if blocks[0] < 2 else True
        @pl.when(inside)
        def _():
            for i in blocks:
                copy = relay_copy(k, i)
                copy.wait_recv()
                copy.start()

    lane = lax.broadcasted_iota(jnp.int32, (side, LANES), 1)
    real = lane < chunk
    for n in ("ctf", "pick", "defocus"):
        loads[n].wait()
    for i in range(count):
        taken = dot(ctf[defocus[i]], pick[...]).astype(jnp.bfloat16)
        for to in range(tiles):
            ctf_out[to, i] = taken[:, to * LANES : (to + 1) * LANES]

    def ctf_copy(i, source):
        to = order[i]
        return pltpu.make_async_remote_copy(
            src_ref=ctf_out.at[to],
            dst_ref=ctf_in.at[source],
            send_sem=ctf_sem.at[0],
            recv_sem=ctf_sem.at[1],
            device_id={"tile": to},
            device_id_type=MESH,
        )

    pl.semaphore_wait(barrier, jnp.where(middle, 11, jnp.where(b == 0, 10, 8)))
    g_sends(lambda c: c.start())
    g_in[b, t] = g_out[t]
    ctf_in[t] = ctf_out[t]

    loads["bank"].wait()
    loads["orient"].wait()
    columns = over_n[:box, pl.ds(pl.multiple_of(t * LANES, LANES), LANES)]
    firsts = []
    for i in range(count):
        image = bank[orient[i]].astype(jnp.float32)
        centre = jnp.sum(image, keepdims=True) * (1.0 / (box * box))
        image = image - centre
        spread = jnp.sum(image * image, keepdims=True) * (1.0 / (box * box))
        scale = 1.0 / (box * jnp.sqrt(spread + 1e-05))
        template = (image * scale).astype(jnp.bfloat16)
        firsts.append(dot(template, columns).astype(jnp.bfloat16))
        if i == 0:
            for dt in (2, 3, 1):
                ctf_copy(dt, t).start()
    @pl.when(ends)
    def _():
        for i in (2, 3):
            arrive(b, i)
            g_pass(i, 0).start()
        for i in (2, 3):
            g_pass(i, 1).start()

        @pl.when(b == 3)
        def _():
            for i in (2, 3):
                g_pass(i, 2).start()

    loads["cs"].wait()
    tmpl = dot(cs[:, :box], jnp.concatenate(firsts, axis=1))
    relay(0, (0,))
    relay(1, (0,))
    relay(0, (1,))
    relay(1, (1,))

    def transform(j):
        spread_in = g_in[j].reshape(side, LANES)
        turned = swap(dot(cs[side:], spread_in))
        straight = dot(cs[:side], spread_in)
        mic[j] = (straight + jnp.where(real, turned, -turned)).astype(jnp.bfloat16)

    @pl.when(middle)
    def _():
        arrive(b, 2)
        arrive(b, 3)

    arrive(b, 1)
    transform(b)
    def rest(j):
        for i in range(tiles):
            arrive(j, i)

    @pl.when(b == 2)
    def _():
        relay(0, (2, 3))
        transform(near)

    @pl.when(b == 1)
    def _():
        relay(0, (2, 3))
        transform(near)

    loads["flip"].wait()
    loads["over_l"].wait()
    drain(ctf_in.at[: tiles - 1], ctf_sem.at[1])
    for i in range(count):
        here = ctf_in[:, i].reshape(side, LANES)
        gain = here.astype(jnp.float32) + swap(dot(flip[...], here))
        gain = jnp.where(real, gain, swap(gain))
        part = tmpl[:, i * LANES : (i + 1) * LANES]
        turned = swap(part[side:])
        value = (part[:side] + jnp.where(real, turned, -turned)) * gain
        other = swap(value)
        spec[i, 0] = jnp.where(real, value, other)
        spec[i, 1] = jnp.where(real, other, -value)

    wave = jnp.concatenate([cs[:lags], cs[side : side + lags]], axis=0)
    real_lag = lax.broadcasted_iota(jnp.int32, (lags, LANES), 1) < chunk

    def correlate(j):
        own = mic[j].astype(jnp.float32)
        turned = swap(own)
        product = jnp.concatenate(
            [(own * spec[i, 0] + turned * spec[i, 1]).astype(jnp.bfloat16) for i in range(count)],
            axis=1,
        )
        both = dot(wave, product) * (1.0 / side)
        lag = []
        for i in range(count):
            part = both[:, i * LANES : (i + 1) * LANES]
            turned = swap(part[lags:])
            lag.append(part[:lags] + jnp.where(real_lag, -turned, turned))
        lag = jnp.concatenate(lag, axis=1).astype(jnp.bfloat16)
        return dot(lag, over_l[...]).astype(jnp.bfloat16).reshape(tiles, lags // tiles, 2 * lags)

    def cor_copy(s, dt, kind):
        to = lax.rem(t + dt, tiles)
        return pltpu.make_async_remote_copy(
            src_ref=cor_out.at[s, to],
            dst_ref=cor_in.at[s, dt],
            send_sem=cor_send.at[kind],
            recv_sem=cor_recv.at[kind],
            device_id={"blk": lax.rem(b + blks - s, blks), "tile": to},
            device_id_type=MESH,
        )

    def one(j):
        s = lax.rem(b + blks - j, blks)
        cor_out[s] = correlate(j)
        for dt in range(tiles):
            cor_copy(s, dt, 1).start()

    cor_out[0] = correlate(b)
    for dt in range(1, tiles):
        cor_copy(0, dt, 0).start()
    cor_in[0, 0] = cor_out[0, t]

    for k, levels in enumerate(((1, 2, 0, 0), (3, 0, 1, 2), (2, 3, 3, 1))):
        j = jnp.where(b < 2, jnp.where(b == 0, levels[0], levels[1]), jnp.where(b == 2, levels[2], levels[3]))
        if k == 0:

            @pl.when(b == 2)
            def _():
                arrive(j, 2)
                arrive(j, 3)

            pl.when(ends)(lambda: rest(j))
            pl.when(b != 1)(lambda: transform(j))
        elif k == 1:

            @pl.when(b != 2)
            def _():
                rest(j)
                transform(j)
        else:

            @pl.when(b == 1)
            def _():
                arrive(j, 2)
                arrive(j, 3)

            pl.when(b != 1)(lambda: rest(j))
            transform(j)
        one(j)
    drain(cor_in.at[0, 1:], cor_recv.at[0])
    drain(cor_in.at[1:], cor_recv.at[1])
    total = jnp.sum(cor_in[...].astype(jnp.float32), axis=1) * (1.0 / side)
    best = jnp.max(total, axis=0)
    summed = jnp.sum(total, axis=0)
    squares = jnp.sum(total * total, axis=0)
    out[0] = jnp.maximum(best, pltpu.roll(best, lags, 1))[:, :lags]
    out[1] = (summed + pltpu.roll(summed, lags, 1))[:, :lags]
    out[2] = (squares + pltpu.roll(squares, lags, 1))[:, :lags]

    drain(g_in.at[0, 1:], g_send.at[1])
    pl.when(b > 0)(lambda: drain(g_in.at[1:, :2], g_send.at[2]))

    @pl.when(b == 0)
    def _():
        drain(g_in.at[0], g_send.at[2])
        drain(g_in.at[1:, :2], g_send.at[0])

    drain(ctf_out.at[: tiles - 1], ctf_sem.at[0])
    drain(cor_out.at[0, 1:], cor_send.at[0])
    drain(cor_out.at[1:], cor_send.at[1])
    pl.when(middle)(lambda: drain(g_in.at[:2], g_send.at[0]))
    pl.when(b == 3)(lambda: drain(g_in.at[0], g_send.at[0]))


def on_device(blks, tiles, pieces, bank, orient_ids, defocus_ids, ctf):
    side, box = pieces.shape[2], bank.shape[1]
    rows, lags, count = side // tiles, side - box, orient_ids.shape[0]
    tables = make_tables(side, box, lags, tiles)
    over_n, cs, pick, flip, over_l = tables
    bf16, dma = jnp.bfloat16, pltpu.SemaphoreType.DMA
    hbm_spec = pl.BlockSpec(memory_space=pltpu.HBM)
    line = blks == 4 and tiles == 4
    loaded = [
        pltpu.SMEM(orient_ids.shape, jnp.int32),
        pltpu.SMEM(defocus_ids.shape, jnp.int32),
        pltpu.VMEM((rows, side), bf16),
        pltpu.VMEM(bank.shape, bf16),
        pltpu.VMEM(ctf.shape, bf16),
        pltpu.VMEM(over_n.shape, bf16),
        pltpu.VMEM(cs.shape, bf16),
        pltpu.VMEM(pick.shape, bf16),
        pltpu.VMEM(flip.shape, bf16),
        pltpu.VMEM(over_l.shape[1:], bf16),
    ]
    gain = [pltpu.VMEM((tiles, count, rows, LANES), bf16)] * 2
    spec = pltpu.VMEM((count, 2, side, LANES), jnp.float32)
    cor = [pltpu.VMEM((blks, tiles, lags // tiles, 2 * lags), bf16)] * 2
    if line:
        body = functools.partial(line_kernel, side, box, lags)
        scratch = [
            *loaded,
            pltpu.VMEM((tiles, rows, LANES), bf16),
            pltpu.VMEM((blks, tiles, rows, LANES), bf16),
            *gain,
            spec,
            pltpu.VMEM((blks, side, LANES), bf16),
            *cor,
            dma((10,)),
            dma((3,)),
            dma((blks, tiles)),
            dma((2,)),
            dma((2,)),
            dma((2,)),
        ]
    else:
        body = functools.partial(kernel, blks, tiles, side, box, lags)
        scratch = [
            *loaded,
            pltpu.VMEM((tiles, rows, LANES), bf16),
            pltpu.VMEM((tiles, rows, LANES), bf16),
            *gain,
            spec,
            pltpu.VMEM((blks, side, LANES), bf16),
            *cor,
            dma((10,)),
            dma((tiles - 1,)),
            dma((tiles - 1,)),
            dma((tiles - 1,)),
            dma((tiles - 1,)),
            dma((blks - 1, PARTS)),
            dma((blks - 1, PARTS)),
            dma((PARTS,)),
            dma((blks, tiles)),
            dma((blks, tiles)),
        ]
    stats = pl.pallas_call(
        body,
        out_shape=pltpu.VMEM((3, lags // tiles, lags), jnp.float32),
        in_specs=[hbm_spec] * 10,
        out_specs=pl.BlockSpec(memory_space=pltpu.VMEM),
        scratch_shapes=scratch,
        compiler_params=pltpu.CompilerParams(
            collective_id=0, has_side_effects=True, vmem_limit_bytes=56 * 2**20
        ),
    )(orient_ids, defocus_ids, pieces, bank, ctf, *tables)
    return stats[0:1], stats[1:2], stats[2:3]


def solution(mesh):
    blks, tiles = mesh.shape["blk"], mesh.shape["tile"]
    placed = (
        P(("grp", "blk"), "tile", None),
        P("blk", None, None),
        P("blk"),
        P(("grp", "blk")),
        P("grp", "tile", None),
    )
    out = P(("grp", "blk"), "tile", None)
    return jax.shard_map(
        functools.partial(on_device, blks, tiles),
        mesh=mesh,
        in_specs=placed,
        out_specs=(out, out, out),
        check_vma=False,
    )
```
